768 devices in a mesh: walker: 12 (over z), orb: 64 (over x, y, core).
Axes of the slice: x: 4, y: 8, z: 12, core: 2. Of those that a mesh axis runs over, the one named last changes fastest.
Arguments:
- occupations: int32 [3072, 128], P(('walker', 'orb')), may hold values from 0 to 255, as said below
- local_energy: float32 [3072], P(('walker', 'orb')), may hold values from -4.5 to -0.5
- embed_weight: bfloat16 [18, 256], replicated, may hold values from -1.5 to 1.5
- conv_weight: bfloat16 [2304, 256], replicated, may hold values from -0.125 to 0.125
- head_weight: bfloat16 [256, 128], replicated, may hold values from -0.375 to 0.375
- a_factor: float32 [256, 256], P('orb'), may hold values from -1 to 2, as said below
- g_factor: float32 [128, 128], replicated, may hold values from -1 to 2, as said below
- a_inverse: float32 [256, 256], P('orb'), may hold values from -1 to 2, as said below
- g_inverse: float32 [128, 128], replicated, may hold values from -1 to 2, as said below
Outputs:
- head_update: float32 [256, 128], P('orb')
- conv_update: float32 [2304, 256], P('orb')
- new_a_factor: float32 [256, 256], P('orb')
- new_g_factor: float32 [128, 128], replicated
The draws below stay inside these ranges and needn't reach their ends.
Inputs may be any that keep to these rules, and one draw needn't show every extreme that they name: `occupations`: in each row the first 64 entries are distinct sites, and so are the last 64. `a_factor`: Symmetric; each diagonal entry exceeds the sum of the magnitudes of the other entries of its row. `g_factor`: Symmetric; each diagonal entry exceeds the sum of the magnitudes of the other entries of its row. `a_inverse`: Symmetric; each diagonal entry exceeds the sum of the magnitudes of the other entries of its row. `g_inverse`: Symmetric; each diagonal entry exceeds the sum of the magnitudes of the other entries of its row.
All inputs are finite; a program needn't handle non-finite values.
Results may differ from the reference program's by a relative error of at most 0.0071.
Values sent between devices are 32-bit elements; how exact they have to be, the bound alone decides.
A program may use at most 64 MiB of HBM per device.

```python
import math
import jax
import jax.numpy as jnp
from jax import lax

L = 16
C = 256
NS_STEPS = 3
NE = 128
SAMPLES = 3072


def symmetric_draw(key, size):
    first_key, second_key = jax.random.split(key)
    diagonal = jnp.exp(jax.random.uniform(first_key, (size,), jnp.float32, 0.0, math.log(2.0)))
    spread_noise = jax.random.uniform(second_key, (size, size), jnp.float32, -1.0, 1.0)
    symmetric = 0.5 * (spread_noise + spread_noise.T) * (0.95 / size)
    identity = jnp.eye(size, dtype=jnp.float32)
    return symmetric * (1.0 - identity) + identity * diagonal


def draw_occupations(key, part):
    sample_keys = jax.random.split(key, SAMPLES)

    def one_sample(sample_key):
        up_sites = jax.random.permutation(jax.random.fold_in(sample_key, 0), L * L)[:NE // 2]
        down_sites = jax.random.permutation(jax.random.fold_in(sample_key, 1), L * L)[:NE // 2]
        return jnp.concatenate([up_sites, down_sites]).astype(jnp.int32)
    return jax.vmap(one_sample)(sample_keys)


def draw_local_energy(key, part):
    energy_ramp = 1.0 + 2.0 * jnp.arange(SAMPLES, dtype=jnp.float32) / max(SAMPLES - 1, 1)
    energy_level = jax.random.uniform(key, (SAMPLES,), jnp.float32, 0.5, 1.5)
    return -energy_ramp * energy_level


def draw_a_factor(key, part):
    return symmetric_draw(jax.random.fold_in(key, 11), C)


def draw_g_factor(key, part):
    return symmetric_draw(jax.random.fold_in(key, 12), NE)


def draw_a_inverse(key, part):
    return symmetric_draw(jax.random.fold_in(key, 13), C)


def draw_g_inverse(key, part):
    return symmetric_draw(jax.random.fold_in(key, 14), NE)


def noise(stream_key, shape, deviation, bound, held_as=jnp.bfloat16):
    result = deviation * jax.random.normal(stream_key, shape, jnp.float32)
    return jnp.clip(result, min=-bound, max=bound).astype(held_as)


def setup_inputs(seed: int = 0) -> dict:
    arg_keys = jax.random.split(jax.random.key(seed), 10)
    occupations = draw_occupations(jax.random.fold_in(arg_keys[9], 71), 0)
    local_energy = draw_local_energy(jax.random.fold_in(arg_keys[9], 71), 0)
    embed_weight = noise(arg_keys[2], (18, C), 18 ** -0.5, 1.5)
    conv_weight = noise(arg_keys[3], (9 * C, C), (9 * C) ** -0.5, 0.125)
    head_weight = noise(arg_keys[4], (C, NE), C ** -0.5, 0.375)
    a_factor = draw_a_factor(jax.random.fold_in(arg_keys[9], 71), 0)
    g_factor = draw_g_factor(jax.random.fold_in(arg_keys[9], 71), 0)
    a_inverse = draw_a_inverse(jax.random.fold_in(arg_keys[9], 71), 0)
    g_inverse = draw_g_inverse(jax.random.fold_in(arg_keys[9], 71), 0)
    return {"occupations": occupations, "local_energy": local_energy, "embed_weight": embed_weight, "conv_weight": conv_weight, "head_weight": head_weight, "a_factor": a_factor, "g_factor": g_factor, "a_inverse": a_inverse, "g_inverse": g_inverse}


decay_rate = 0.8

def neighbours(lattice):
    shifted_views = [jnp.roll(lattice, (-shift_x, -shift_y), axis=(1, 2)) for shift_x in (-1, 0, 1) for shift_y in (-1, 0, 1)]
    return jnp.concatenate(shifted_views, axis=-1)

def forward_backward(occupations, embed_weight, conv_weight, head_weight):
    sample_count = occupations.shape[0]
    site_count = L * L
    site_ids = jnp.arange(site_count, dtype=jnp.int32)
    select = (occupations[:, :, None] == site_ids[None, None, :]).astype(jnp.float32)
    half_count = NE // 2
    up_fill = lax.optimization_barrier(jnp.sum(select[:, :half_count], axis=1))
    down_fill = lax.optimization_barrier(jnp.sum(select[:, half_count:], axis=1))
    lattice = jnp.stack([up_fill, down_fill], axis=-1).reshape(sample_count, L, L, 2).astype(jnp.bfloat16)
    embed_in = neighbours(lattice).reshape(sample_count * site_count, 18)
    embedded = jnp.tanh(jnp.dot(embed_in, embed_weight, preferred_element_type=jnp.float32)).astype(jnp.bfloat16)
    patches = neighbours(embedded.reshape(sample_count, L, L, C)).reshape(sample_count, site_count, 9 * C)
    conv_pre = jnp.dot(patches.reshape(sample_count * site_count, 9 * C), conv_weight, preferred_element_type=jnp.float32)
    squash = jnp.tanh(conv_pre)
    hidden = (embedded.astype(jnp.float32) + squash).astype(jnp.bfloat16).reshape(sample_count, site_count, C)
    electron_rows = jnp.einsum('bis,bsc->bic', select, hidden.astype(jnp.float32), precision=lax.Precision.HIGHEST).astype(jnp.bfloat16)
    logits = jnp.dot(electron_rows.reshape(sample_count * NE, C), head_weight, preferred_element_type=jnp.float32).reshape(sample_count, NE, NE)
    orbital_tanh = jnp.tanh(logits)
    identity = jnp.eye(NE, dtype=jnp.float32)
    slater_scale = 0.35 / math.sqrt(NE)
    slater = identity + slater_scale * orbital_tanh
    inverse_est = jnp.broadcast_to(identity, slater.shape)
    for sweep in range(NS_STEPS):
        product = jnp.einsum('bij,bjk->bik', slater, inverse_est, precision=lax.Precision.HIGHEST)
        inverse_est = jnp.einsum('bij,bjk->bik', inverse_est, 2.0 * identity - product, precision=lax.Precision.HIGHEST)
    log_grads = (1.0 - orbital_tanh * orbital_tanh) * jnp.swapaxes(inverse_est, 1, 2)
    cotangent = (slater_scale * log_grads).astype(jnp.bfloat16)
    head_terms = jnp.einsum('bic,bij->bcj', electron_rows.astype(jnp.float32), cotangent.astype(jnp.float32), precision=lax.Precision.HIGHEST)
    flat_rows = electron_rows.reshape(sample_count * NE, C)
    input_gram = jnp.dot(flat_rows.T, flat_rows, preferred_element_type=jnp.float32)
    output_gram = jnp.einsum('bik,bil->kl', log_grads, log_grads, precision=lax.Precision.HIGHEST)
    row_grads = jnp.dot(cotangent.reshape(sample_count * NE, NE), head_weight.T, preferred_element_type=jnp.float32).astype(jnp.bfloat16).reshape(sample_count, NE, C)
    hidden_grad = jnp.einsum('bis,bic->bsc', select, row_grads.astype(jnp.float32), precision=lax.Precision.HIGHEST)
    pre_grad = (hidden_grad.reshape(sample_count * site_count, C) * (1.0 - squash * squash)).astype(jnp.bfloat16).reshape(sample_count, site_count, C)
    conv_terms = jnp.einsum('bsk,bsc->bkc', patches.astype(jnp.float32), pre_grad.astype(jnp.float32), precision=lax.Precision.HIGHEST)
    return (input_gram, output_gram, head_terms, conv_terms)

def reference(occupations, local_energy, embed_weight, conv_weight, head_weight, a_factor, g_factor, a_inverse, g_inverse):
    mean_energy = jnp.mean(local_energy)
    weights = (local_energy - mean_energy) / SAMPLES
    block_size = math.gcd(SAMPLES, 8)
    block_count = SAMPLES // block_size
    occ_blocks = occupations.reshape(block_count, block_size, NE)
    weight_blocks = weights.reshape(block_count, block_size)

    def accumulate(carry, inputs):
        occ_block, weight_block = inputs
        input_gram, output_gram, head_terms, conv_terms = forward_backward(occ_block, embed_weight, conv_weight, head_weight)
        head_part = lax.optimization_barrier(jnp.sum(weight_block[:, None, None] * head_terms, axis=0))
        conv_part = lax.optimization_barrier(jnp.sum(weight_block[:, None, None] * conv_terms, axis=0))
        return ((carry[0] + input_gram, carry[1] + output_gram, carry[2] + head_part, carry[3] + conv_part), None)
    initial = (jnp.zeros((C, C), jnp.float32), jnp.zeros((NE, NE), jnp.float32), jnp.zeros((C, NE), jnp.float32), jnp.zeros((9 * C, C), jnp.float32))
    totals, unused = lax.scan(accumulate, initial, (occ_blocks, weight_blocks))
    input_gram, output_gram, head_grad, conv_grad = totals
    new_a_factor = decay_rate * a_factor + (1.0 - decay_rate) * input_gram / (SAMPLES * NE)
    new_g_factor = decay_rate * g_factor + (1.0 - decay_rate) * output_gram / SAMPLES
    precond = jnp.dot(jnp.dot(a_inverse, head_grad, precision=lax.Precision.HIGHEST), g_inverse, precision=lax.Precision.HIGHEST)
    head_norm = jnp.sum(precond * head_grad)
    conv_norm = jnp.sum(conv_grad * conv_grad)
    head_update = -jnp.sqrt(C * NE / 4.0 / head_norm) * precond
    conv_update = -jnp.sqrt(9 * C * C / 4.0 / conv_norm) * conv_grad
    return (head_update, conv_update, new_a_factor, new_g_factor)
```

```python
import functools
import math

import jax
import jax.numpy as jnp
from jax import lax
from jax.experimental import pallas as pl
from jax.experimental.pallas import tpu as pltpu
from jax.sharding import PartitionSpec as P

L = 16
C = 256
NS_STEPS = 3
NE = 128
X_CHIPS = 4
TILES = 11

decay_rate = 0.8
MESH = pl.DeviceIdType.MESH


class Place:
    def __init__(self, nx, ny, nz):
        self.nx, self.ny, self.nz = nx, ny, nz
        self.z = lax.axis_index("walker")
        self.orb = lax.axis_index("orb")
        self.c = lax.rem(self.orb, 2)
        self.y = lax.rem(lax.div(self.orb, 2), ny)
        self.x = lax.div(self.orb, 2 * ny)
        self.k = self.x * 2 + self.c

    def at(self, x, y, c):
        return (self.z, (x * self.ny + y) * 2 + c)

    def core(self):
        return self.at(self.x, self.y, 1 - self.c)

    def along_x(self, d):
        return self.at(lax.rem(self.x + d, self.nx), self.y, self.c)

    def along_y(self, d):
        return self.at(self.x, lax.rem(self.y + d, self.ny), self.c)

    def along_k(self, d):
        k = lax.rem(self.k + d, 2 * self.nx)
        return self.at(lax.div(k, 2), self.y, lax.rem(k, 2))

    def along_z(self, d):
        return (lax.rem(self.z + d, self.nz), self.orb)

    def greet(self):
        barrier = pltpu.get_barrier_semaphore()
        peers = [self.along_y(d) for d in range(1, self.ny)]
        peers += [self.along_k(d) for d in range(1, 2 * self.nx)]
        peers += [self.along_z(d) for d in range(1, self.nz)]
        for peer in peers:
            pl.semaphore_signal(barrier, inc=1, device_id=peer, device_id_type=MESH)
        pl.semaphore_wait(barrier, len(peers))


class Sender:
    def __init__(self, send_sem, recv_sem):
        self.send_sem, self.recv_sem, self.used = send_sem, recv_sem, 0

    def __call__(self, source, target, device):
        copy = pltpu.make_async_remote_copy(
            src_ref=source,
            dst_ref=target,
            send_sem=self.send_sem.at[self.used],
            recv_sem=self.recv_sem.at[self.used],
            device_id=device,
            device_id_type=MESH,
        )
        copy.start()
        self.used += 1
        return copy


def wait_all(copies):
    for copy in copies:
        copy.wait()


def total_of(first, ref, count):
    total = first
    for i in range(count):
        total = total + ref[i]
    return total


def spread(place, slots_ref, out_ref):
    for i in range(2 * place.nx):
        k = lax.rem(place.k - i + 2 * place.nx, 2 * place.nx)
        for j in range(place.ny):
            y = lax.rem(place.y - j + place.ny, place.ny)
            out_ref[k, y] = slots_ref[i, j]


def gather_kernel(
    nx, ny, nz, rows_ref, energy_ref, gathered_ref, total_ref,
    rows_y, rows_k, energy_y, energy_k, energy_z, part_k, part_z, send_sem, recv_sem,
):
    place = Place(nx, ny, nz)
    place.greet()
    send = Sender(send_sem, recv_sem)
    energies = [send(energy_ref, energy_y.at[d - 1], place.along_y(d)) for d in range(1, ny)]
    rows = [send(rows_ref, rows_y.at[d], place.along_y(d)) for d in range(1, ny)]
    rows_y[0] = rows_ref[...]
    wait_all(energies)
    part_k[...] = total_of(energy_ref[...], energy_y, ny - 1)
    energies = [send(part_k, energy_k.at[d - 1], place.along_k(d)) for d in range(1, 2 * nx)]
    wait_all(rows)
    rows = [send(rows_y, rows_k.at[d], place.along_k(d)) for d in range(1, 2 * nx)]
    rows_k[0] = rows_y[...]
    wait_all(energies)
    part_z[...] = total_of(part_k[...], energy_k, 2 * nx - 1)
    energies = [send(part_z, energy_z.at[d - 1], place.along_z(d)) for d in range(1, nz)]
    wait_all(rows)
    spread(place, rows_k, gathered_ref)
    wait_all(energies)
    total_ref[...] = total_of(part_z[...], energy_z, nz - 1)


def gather(nx, ny, nz, rows, energy):
    tile = (8, 128)
    copies = 2 * (ny - 1) + 2 * (2 * nx - 1) + nz - 1
    return pl.pallas_call(
        functools.partial(gather_kernel, nx, ny, nz),
        name="gather_rows",
        out_shape=(
            jax.ShapeDtypeStruct((2 * nx, ny) + tile, jnp.float32),
            jax.ShapeDtypeStruct(tile, jnp.float32),
        ),
        in_specs=[pl.BlockSpec(memory_space=pltpu.VMEM)] * 2,
        out_specs=[pl.BlockSpec(memory_space=pltpu.VMEM)] * 2,
        scratch_shapes=[
            pltpu.VMEM((ny,) + tile, jnp.float32),
            pltpu.VMEM((2 * nx, ny) + tile, jnp.float32),
            pltpu.VMEM((ny - 1,) + tile, jnp.float32),
            pltpu.VMEM((2 * nx - 1,) + tile, jnp.float32),
            pltpu.VMEM((nz - 1,) + tile, jnp.float32),
            pltpu.VMEM(tile, jnp.float32),
            pltpu.VMEM(tile, jnp.float32),
            pltpu.SemaphoreType.DMA((copies,)),
            pltpu.SemaphoreType.DMA((copies,)),
        ],
        compiler_params=pltpu.CompilerParams(collective_id=0, has_side_effects=True),
    )(rows, energy)


def reduce_kernel(
    nx, ny, nz, parts_ref, chunk_ref, gathered_ref,
    from_core, sum_core, from_x, sum_x, from_y, sum_y, from_z, sum_z, got_z,
    block, block_y, block_k, send_sem, recv_sem,
):
    place = Place(nx, ny, nz)
    place.greet()
    send = Sender(send_sem, recv_sem)
    order = [*range(1, nx), 0]
    other = 1 - place.c
    at_x = [lax.rem(place.x + d, nx) for d in order]
    copies = [send(parts_ref.at[other, i], from_core.at[i], place.core()) for i in at_x]
    sent = []
    for d, i, copy in zip(order, at_x, copies):
        copy.wait()
        sum_core[i] = parts_ref[place.c, i] + from_core[i]
        if d:
            sent.append(send(sum_core.at[i], from_x.at[d - 1], place.along_x(d)))
    wait_all(sent)
    sum_x[...] = total_of(sum_core[place.x], from_x, nx - 1)
    wait_all(
        [
            send(sum_x.at[lax.rem(place.y + d, ny)], from_y.at[d - 1], place.along_y(d))
            for d in range(1, ny)
        ]
    )
    sum_y[...] = jnp.zeros_like(sum_y)
    sum_y[0:TILES] = total_of(sum_x[place.y], from_y, ny - 1)
    wait_all(
        [
            send(sum_y.at[lax.rem(place.z + d, nz)], from_z.at[d - 1], place.along_z(d))
            for d in range(1, nz)
        ]
    )
    sum_z[...] = total_of(sum_y[place.z], from_z, nz - 1)
    copies = [send(sum_z, got_z.at[d], place.along_z(d)) for d in range(1, nz)]
    chunk_ref[place.z] = sum_z[...]
    wait_all(copies)
    for d in range(1, nz):
        chunk_ref[lax.rem(place.z - d + nz, nz)] = got_z[d]
    conv = chunk_ref[0:9]
    squares = jnp.sum(jnp.sum(conv * conv, axis=0), axis=0, keepdims=True)
    row = lax.broadcasted_iota(jnp.int32, (8, 128), 0)
    block[...] = jnp.where(row == 6, jnp.broadcast_to(squares, (8, 128)), chunk_ref[TILES - 1])
    copies = [send(block, block_y.at[d], place.along_y(d)) for d in range(1, ny)]
    block_y[0] = block[...]
    wait_all(copies)
    copies = [send(block_y, block_k.at[d], place.along_k(d)) for d in range(1, 2 * nx)]
    block_k[0] = block_y[...]
    wait_all(copies)
    spread(place, block_k, gathered_ref)


def reduce(nx, ny, nz, parts):
    tile = (8, 128)
    copies = nx + (nx - 1) + 2 * (ny - 1) + 2 * (nz - 1) + 2 * nx - 1

    def buffer(*lead):
        return pltpu.VMEM(lead + tile, jnp.float32)

    return pl.pallas_call(
        functools.partial(reduce_kernel, nx, ny, nz),
        name="reduce_parts",
        out_shape=(
            jax.ShapeDtypeStruct((nz,) + tile, jnp.float32),
            jax.ShapeDtypeStruct((2 * nx, ny) + tile, jnp.float32),
        ),
        in_specs=[pl.BlockSpec(memory_space=pltpu.VMEM)],
        out_specs=[pl.BlockSpec(memory_space=pltpu.VMEM)] * 2,
        scratch_shapes=[
            buffer(nx, ny, TILES),
            buffer(nx, ny, TILES),
            buffer(nx - 1, ny, TILES),
            buffer(ny, TILES),
            buffer(ny - 1, TILES),
            buffer(nz),
            buffer(nz - 1),
            buffer(),
            buffer(nz),
            buffer(),
            buffer(ny),
            buffer(2 * nx, ny),
            pltpu.SemaphoreType.DMA((copies,)),
            pltpu.SemaphoreType.DMA((copies,)),
        ],
        compiler_params=pltpu.CompilerParams(collective_id=1, has_side_effects=True),
    )(parts)


def by_place(nx, ny, array, width):
    rows = array.shape[0] // (2 * nx * ny)
    split = array.reshape(nx, ny, 2, rows, width // 128, 128)
    return split.transpose(2, 0, 1, 4, 3, 5).reshape(2, nx, ny, rows * width // 128, 128)


def in_order(nx, ny, gathered):
    split = gathered.reshape(nx, 2, ny, gathered.shape[-2], 128)
    return split.transpose(0, 2, 1, 3, 4).reshape(2 * nx * ny, gathered.shape[-2], 128)


def widen(rows):
    half = rows.shape[-2] // 2
    return jnp.concatenate([rows[..., :half, :], rows[..., half:, :]], axis=-1)


def neighbours(lattice):
    shifted_views = [
        jnp.roll(lattice, (-shift_x, -shift_y), axis=(1, 2))
        for shift_x in (-1, 0, 1)
        for shift_y in (-1, 0, 1)
    ]
    return jnp.concatenate(shifted_views, axis=-1)


def local_parts(occupations, weights, embed_weight, conv_weight, head_weight):
    sample_count = occupations.shape[0]
    site_count = L * L
    site_ids = jnp.arange(site_count, dtype=jnp.int32)
    select = (occupations[:, :, None] == site_ids[None, None, :]).astype(jnp.bfloat16)
    half_count = NE // 2
    up_fill = jnp.sum(select[:, :half_count].astype(jnp.float32), axis=1)
    down_fill = jnp.sum(select[:, half_count:].astype(jnp.float32), axis=1)
    lattice = (
        jnp.stack([up_fill, down_fill], axis=-1).reshape(sample_count, L, L, 2).astype(jnp.bfloat16)
    )
    embed_in = neighbours(lattice).reshape(sample_count * site_count, 18)
    embedded = jnp.tanh(jnp.dot(embed_in, embed_weight, preferred_element_type=jnp.float32)).astype(
        jnp.bfloat16
    )
    patches = neighbours(embedded.reshape(sample_count, L, L, C)).reshape(
        sample_count * site_count, 9 * C
    )
    conv_pre = jnp.dot(patches, conv_weight, preferred_element_type=jnp.float32)
    squash = jnp.tanh(conv_pre)
    hidden = (
        (embedded.astype(jnp.float32) + squash)
        .astype(jnp.bfloat16)
        .reshape(sample_count, site_count, C)
    )
    electron_rows = jnp.einsum(
        "bis,bsc->bic", select, hidden, preferred_element_type=jnp.float32
    ).astype(jnp.bfloat16)
    flat_rows = electron_rows.reshape(sample_count * NE, C)
    logits = jnp.dot(flat_rows, head_weight, preferred_element_type=jnp.float32).reshape(
        sample_count, NE, NE
    )
    orbital_tanh = jnp.tanh(logits)
    identity = jnp.eye(NE, dtype=jnp.float32)
    slater_scale = 0.35 / math.sqrt(NE)
    slater = identity + slater_scale * orbital_tanh
    inverse_est = 2.0 * identity - slater
    for sweep in range(NS_STEPS - 1):
        product = jnp.einsum("bij,bjk->bik", slater, inverse_est, precision=lax.Precision.HIGHEST)
        inverse_est = jnp.einsum(
            "bij,bjk->bik", inverse_est, 2.0 * identity - product, precision=lax.Precision.HIGHEST
        )
    log_grads = (1.0 - orbital_tanh * orbital_tanh) * jnp.swapaxes(inverse_est, 1, 2)
    cotangent = (slater_scale * log_grads).astype(jnp.bfloat16)
    weighted = (weights[:, None, None] * (slater_scale * log_grads)).astype(jnp.bfloat16)
    head_part = jnp.dot(
        flat_rows.T, weighted.reshape(sample_count * NE, NE), preferred_element_type=jnp.float32
    )
    input_gram = jnp.einsum("nc,nd->cd", flat_rows, flat_rows, preferred_element_type=jnp.float32)
    flat_grads = log_grads.reshape(sample_count * NE, NE)
    output_gram = jnp.dot(flat_grads.T, flat_grads, precision=lax.Precision.HIGHEST)
    row_grads = (
        jnp.dot(
            cotangent.reshape(sample_count * NE, NE),
            head_weight.T,
            preferred_element_type=jnp.float32,
        )
        .astype(jnp.bfloat16)
        .reshape(sample_count, NE, C)
    )
    hidden_grad = jnp.einsum("bis,bic->bsc", select, row_grads, preferred_element_type=jnp.float32)
    pre_grad = (
        (weights[:, None, None] * hidden_grad).reshape(sample_count * site_count, C)
        * (1.0 - squash * squash)
    ).astype(jnp.bfloat16)
    conv_part = jnp.dot(patches.T, pre_grad, preferred_element_type=jnp.float32)
    return conv_part, input_gram, head_part, output_gram


def per_device(
    nx,
    ny,
    nz,
    occupations,
    local_energy,
    embed_weight,
    conv_weight,
    head_weight,
    a_factor,
    g_factor,
    a_inverse,
    g_inverse,
):
    samples_all = occupations.shape[0] * 2 * nx * ny * nz
    inverse_tile = jnp.concatenate([a_inverse[:, :128], a_inverse[:, 128:]], axis=0)
    energy_tile = jnp.broadcast_to(jnp.sum(local_energy), (8, 128))
    inverse_tiles, energy_whole = gather(nx, ny, nz, inverse_tile, energy_tile)
    mean_energy = energy_whole[0, 0] / samples_all
    weights = (local_energy - mean_energy) / samples_all
    conv_part, input_gram, head_part, output_gram = local_parts(
        occupations, weights, embed_weight, conv_weight, head_weight
    )
    output_rows = by_place(nx, ny, output_gram, NE)
    parts = jnp.concatenate(
        [
            by_place(nx, ny, conv_part, C),
            by_place(nx, ny, input_gram, C),
            by_place(nx, ny, head_part, NE),
            jnp.pad(output_rows, ((0, 0),) * 3 + ((0, 4 - output_rows.shape[3]), (0, 0))),
        ],
        axis=3,
    ).reshape(2, nx, ny, TILES, 8, 128)
    chunk, gathered = reduce(nx, ny, nz, parts)
    chunk = chunk.reshape(nz * 8, 128)
    conv_panel = widen(chunk[:72])
    input_rows = widen(chunk[72:80])
    blocks = in_order(nx, ny, gathered)
    head_grad = blocks[:, 0:4].reshape(C, NE)
    output_sum = blocks[:, 4:6].reshape(NE, NE)
    conv_norm = jnp.sum(blocks[:, 6])
    inverse_whole = widen(in_order(nx, ny, inverse_tiles)).reshape(C, C)
    left_applied = jnp.dot(inverse_whole, head_grad, precision=lax.Precision.HIGHEST)
    precond = jnp.dot(left_applied, g_inverse, precision=lax.Precision.HIGHEST)
    head_norm = jnp.sum(precond * head_grad)
    head_rows = C // (2 * nx * ny)
    precond_rows = lax.dynamic_slice_in_dim(
        precond, lax.axis_index("orb") * head_rows, head_rows, 0
    )
    head_update = -jnp.sqrt(C * NE / 4.0 / head_norm) * precond_rows
    conv_update = -jnp.sqrt(9 * C * C / 4.0 / conv_norm) * conv_panel
    new_a_factor = decay_rate * a_factor + (1.0 - decay_rate) * input_rows / (samples_all * NE)
    new_g_factor = decay_rate * g_factor + (1.0 - decay_rate) * output_sum / samples_all
    return (head_update, conv_update, new_a_factor, new_g_factor)


def solution(mesh):
    nz, orb = mesh.shape["walker"], mesh.shape["orb"]
    in_specs = (
        P(("walker", "orb"), None),
        P(("walker", "orb")),
        P(),
        P(),
        P(),
        P("orb", None),
        P(),
        P("orb", None),
        P(),
    )
    out_specs = (P("orb", None), P("orb", None), P("orb", None), P())
    return jax.shard_map(
        functools.partial(per_device, X_CHIPS, orb // (2 * X_CHIPS), nz),
        mesh=mesh,
        in_specs=in_specs,
        out_specs=out_specs,
        check_vma=False,
    )
```

```python
import functools
import math

import jax
import jax.numpy as jnp
from jax import lax
from jax.experimental import pallas as pl
from jax.experimental.pallas import tpu as pltpu
from jax.sharding import PartitionSpec as P

L = 16
C = 256
NS_STEPS = 3
NE = 128
X_CHIPS = 4
TILES = 11

decay_rate = 0.8
MESH = pl.DeviceIdType.MESH


class Place:
    def __init__(self, nx, ny, nz):
        self.nx, self.ny, self.nz = nx, ny, nz
        self.z = lax.axis_index("walker")
        self.orb = lax.axis_index("orb")
        self.c = lax.rem(self.orb, 2)
        self.y = lax.rem(lax.div(self.orb, 2), ny)
        self.x = lax.div(self.orb, 2 * ny)
        self.k = self.x * 2 + self.c

    def at(self, x, y, c):
        return (self.z, (x * self.ny + y) * 2 + c)

    def core(self):
        return self.at(self.x, self.y, 1 - self.c)

    def along_x(self, d):
        return self.at(lax.rem(self.x + d, self.nx), self.y, self.c)

    def along_y(self, d):
        return self.at(self.x, lax.rem(self.y + d, self.ny), self.c)

    def along_k(self, d):
        k = lax.rem(self.k + d, 2 * self.nx)
        return self.at(lax.div(k, 2), self.y, lax.rem(k, 2))

    def along_z(self, d):
        return (lax.rem(self.z + d, self.nz), self.orb)

    def signal_peers(self):
        barrier = pltpu.get_barrier_semaphore()
        peers = [self.along_y(d) for d in range(1, self.ny)]
        peers += [self.along_k(d) for d in range(1, 2 * self.nx)]
        peers += [self.along_z(d) for d in range(1, self.nz)]
        for peer in peers:
            pl.semaphore_signal(barrier, inc=1, device_id=peer, device_id_type=MESH)
        return len(peers)

    def wait_peers(self, count):
        pl.semaphore_wait(pltpu.get_barrier_semaphore(), count)


class Sender:
    def __init__(self, send_sem, recv_sem):
        self.send_sem, self.recv_sem, self.used = send_sem, recv_sem, 0

    def __call__(self, source, target, device):
        copy = pltpu.make_async_remote_copy(
            src_ref=source,
            dst_ref=target,
            send_sem=self.send_sem.at[self.used],
            recv_sem=self.recv_sem.at[self.used],
            device_id=device,
            device_id_type=MESH,
        )
        copy.start()
        self.used += 1
        return copy


def wait_all(copies):
    for copy in copies:
        copy.wait()


def total_of(first, ref, count):
    total = first
    for i in range(count):
        total = total + ref[i]
    return total


def spread(place, slots_ref, out_ref):
    for i in range(2 * place.nx):
        k = lax.rem(place.k - i + 2 * place.nx, 2 * place.nx)
        for j in range(place.ny):
            y = lax.rem(place.y - j + place.ny, place.ny)
            out_ref[k, y] = slots_ref[i, j]


def site_shift_y(field, b):
    if b == 0:
        return field
    y = lax.broadcasted_iota(jnp.int32, field.shape, 0) & (L - 1)
    sites = field.shape[0]
    if b == 1:
        edge, inside = pltpu.roll(field, L - 1, 0), pltpu.roll(field, sites - 1, 0)
        return jnp.where(y == L - 1, edge, inside)
    edge, inside = pltpu.roll(field, sites - L + 1, 0), pltpu.roll(field, 1, 0)
    return jnp.where(y == 0, edge, inside)


def site_shift_x(field, a):
    if a == 0:
        return field
    cut = L if a == 1 else field.shape[0] - L
    return jnp.concatenate([field[cut:], field[:cut]], axis=0)


def site_patches(field, sign):
    by_y = {b: site_shift_y(field, sign * b).astype(jnp.bfloat16) for b in (-1, 0, 1)}
    return jnp.concatenate(
        [site_shift_x(by_y[b], sign * a) for a in (-1, 0, 1) for b in (-1, 0, 1)], axis=1
    )


def multiply(left, right):
    return jnp.dot(
        left.astype(jnp.bfloat16), right.astype(jnp.bfloat16), preferred_element_type=jnp.float32
    )


def electrons_by_site(occ_ref, b):
    sites = lax.broadcasted_iota(jnp.int32, (L * L, NE), 0)
    return (sites == occ_ref[b]).astype(jnp.float32).astype(jnp.bfloat16)


def forward(b, occ_ref, occ_t_ref, embed_ref, conv_w_ref, head_w_ref,
            embedded_ref, slope_ref, rows_ref, log_ref):
    by_site = electrons_by_site(occ_ref, b)
    electron = lax.broadcasted_iota(jnp.int32, (NE, 128), 0)
    lane = lax.broadcasted_iota(jnp.int32, (NE, 128), 1)
    down = (electron >= NE // 2).astype(jnp.int32)
    spin = ((lane & 1) == down).astype(jnp.float32)
    counts = multiply(by_site, spin)
    tap_of_lane = lax.broadcasted_iota(jnp.int32, counts.shape, 1) >> 1
    near = jnp.zeros_like(counts)
    for j in (-1, 0, 1):
        at_y = site_shift_y(counts, j)
        for i in (-1, 0, 1):
            tap = (i + 1) * 3 + j + 1
            near = jnp.where(tap_of_lane == tap, site_shift_x(at_y, i), near)
    embedded = jnp.tanh(multiply(near, embed_ref[...])).astype(jnp.bfloat16)
    embedded_ref[b] = embedded
    wide = embedded.astype(jnp.float32)
    squash = jnp.tanh(multiply(site_patches(wide, 1), conv_w_ref[...]))
    slope_ref[b] = 1.0 - squash * squash
    hidden = (wide + squash).astype(jnp.bfloat16)
    sites = lax.broadcasted_iota(jnp.int32, (NE, L * L), 1)
    select = (occ_t_ref[b] == sites).astype(jnp.float32)
    rows = multiply(select, hidden).astype(jnp.bfloat16)
    rows_ref[b] = rows
    orbital_tanh = jnp.tanh(multiply(rows, head_w_ref[...]))
    shift = (0.35 / math.sqrt(NE)) * orbital_tanh
    row = lax.broadcasted_iota(jnp.int32, (NE, NE), 0)
    column = lax.broadcasted_iota(jnp.int32, (NE, NE), 1)
    identity = (row == column).astype(jnp.float32)
    second = multiply(shift, shift)
    inverse_est = identity - shift + second - multiply(shift, second)
    inverse_est = inverse_est + multiply(inverse_est, multiply(second, second))
    log_ref[b] = (1.0 - orbital_tanh * orbital_tanh) * inverse_est.T


def backward(b, occ_ref, head_w_ref, slope_ref, log_ref, cot_ref, pre_ref):
    cotangent = ((0.35 / math.sqrt(NE)) * log_ref[b]).astype(jnp.bfloat16)
    cot_ref[b] = cotangent
    row_grads = lax.dot_general(
        cotangent, head_w_ref[...], (((1,), (1,)), ((), ())), preferred_element_type=jnp.float32
    ).astype(jnp.bfloat16)
    hidden_grad = multiply(electrons_by_site(occ_ref, b), row_grads)
    pre_ref[b] = (hidden_grad * slope_ref[b]).astype(jnp.bfloat16)


def grams(samples, rows_ref, log_ref, rows_t_ref, input_ref, output_ref):
    rows = rows_ref[...].reshape(samples * NE, C)
    rows_t = rows.astype(jnp.float32).T.astype(jnp.bfloat16)
    rows_t_ref[...] = rows_t
    input_ref[...] = multiply(rows_t, rows)
    logs = log_ref[...].reshape(samples * NE, NE)
    output_ref[...] = jnp.dot(
        logs.T, logs, precision=lax.Precision.HIGHEST, preferred_element_type=jnp.float32
    )


def weighted_sums(samples, weight_of, embedded_ref, pre_ref, rows_t_ref, cot_ref, conv_ref, head_ref):
    for b in range(samples):
        weight = weight_of(b)
        wide = jnp.concatenate([weight, weight], axis=1)
        embedded_t = embedded_ref[b].astype(jnp.float32).T
        terms = multiply(embedded_t, site_patches(pre_ref[b].astype(jnp.float32), -1))
        head = weight * multiply(rows_t_ref[:, b * NE : (b + 1) * NE], cot_ref[b])
        head_ref[...] = head if b == 0 else head_ref[...] + head
        for tap in range(9):
            rows = slice(tap * C, (tap + 1) * C)
            term = wide * terms[:, rows]
            conv_ref[rows, :] = term if b == 0 else conv_ref[rows, :] + term


def lay_out(nx, ny, conv_ref, input_ref, head_ref, output_ref, parts_ref):
    row = lax.broadcasted_iota(jnp.int32, (8, 128), 0)

    def halves(first, second, c):
        if c == 0:
            return jnp.where(row < 4, first, pltpu.roll(second, 4, 0))
        return jnp.where(row < 4, pltpu.roll(first, 4, 0), second)

    for pair in range(nx * ny):
        x, y = pair // ny, pair % ny
        for c in range(2):
            top = 72 * pair + 40 * c
            for half in range(2):
                lanes = slice(128 * half, 128 * half + 128)
                for i in range(4):
                    tile = conv_ref[top + 8 * i : top + 8 * i + 8, lanes]
                    parts_ref[c, x, y, 4 * half + i] = tile
            middle = slice(72 * pair + 32, 72 * pair + 40)
            parts_ref[c, x, y, 8] = halves(conv_ref[middle, :128], conv_ref[middle, 128:], c)
            eight = slice(8 * pair, 8 * pair + 8)
            parts_ref[c, x, y, 9] = halves(input_ref[eight, :128], input_ref[eight, 128:], c)
            place = 4 * (pair % 2) + 2 * c
            output = output_ref[8 * (pair // 2) : 8 * (pair // 2) + 8, :]
            output = pltpu.roll(output, (4 - place) % 8, 0) if place != 4 else output
            head = head_ref[eight, :] if c == 0 else pltpu.roll(head_ref[eight, :], 4, 0)
            parts_ref[c, x, y, 10] = jnp.where(row < 4, head, output)


def parts_kernel(
    nx, ny, nz, samples,
    occ_ref, occ_t_ref, energy_ref, inverse_ref, embed_ref, conv_w_ref, head_w_ref,
    parts_ref, gathered_ref,
    rows_y, rows_k, energy_own, energy_y, energy_k, energy_z, part_k, part_z,
    embedded_ref, slope_ref, rows_ref, log_ref, cot_ref, pre_ref, rows_t_ref,
    input_ref, output_ref, conv_ref, head_ref, send_sem, recv_sem,
):
    place = Place(nx, ny, nz)
    energy_own[...] = total_of(energy_ref[0], energy_ref.at[1:], samples - 1)
    peers = place.signal_peers()

    def sample(b):
        forward(b, occ_ref, occ_t_ref, embed_ref, conv_w_ref, head_w_ref,
                embedded_ref, slope_ref, rows_ref, log_ref)

    send = Sender(send_sem, recv_sem)
    sample(0)
    place.wait_peers(peers)
    energies = [send(energy_own, energy_y.at[d - 1], place.along_y(d)) for d in range(1, ny)]
    rows = [send(inverse_ref, rows_y.at[d], place.along_y(d)) for d in range(1, ny)]
    rows_y[0] = inverse_ref[...]
    sample(1)
    wait_all(energies)
    part_k[...] = total_of(energy_own[...], energy_y, ny - 1)
    energies = [send(part_k, energy_k.at[d - 1], place.along_k(d)) for d in range(1, 2 * nx)]
    wait_all(rows)
    rows = [send(rows_y, rows_k.at[d], place.along_k(d)) for d in range(1, 2 * nx)]
    rows_k[0] = rows_y[...]
    for b in range(2, samples):
        sample(b)
    wait_all(energies)
    part_z[...] = total_of(part_k[...], energy_k, 2 * nx - 1)
    energies = [send(part_z, energy_z.at[d - 1], place.along_z(d)) for d in range(1, nz)]
    for b in range(samples):
        backward(b, occ_ref, head_w_ref, slope_ref, log_ref, cot_ref, pre_ref)
    grams(samples, rows_ref, log_ref, rows_t_ref, input_ref, output_ref)
    wait_all(rows)
    spread(place, rows_k, gathered_ref)
    wait_all(energies)
    total = total_of(part_z[...], energy_z, nz - 1)[0:1]
    samples_all = samples * 2 * nx * ny * nz
    mean_energy = total / samples_all
    weighted_sums(
        samples,
        lambda b: (energy_ref[b][0:1] - mean_energy) / samples_all,
        embedded_ref, pre_ref, rows_t_ref, cot_ref, conv_ref, head_ref,
    )
    lay_out(nx, ny, conv_ref, input_ref, head_ref, output_ref, parts_ref)


def local_parts(nx, ny, nz, occupations, energy, inverse_tile, embed_weight, conv_weight, head_weight):
    tile = (8, 128)
    samples = occupations.shape[0]
    sites = L * L
    copies = 2 * (ny - 1) + 2 * (2 * nx - 1) + nz - 1

    def buffer(*shape, dtype=jnp.float32):
        return pltpu.VMEM(shape, dtype)

    return pl.pallas_call(
        functools.partial(parts_kernel, nx, ny, nz, samples),
        name="local_parts",
        out_shape=(
            jax.ShapeDtypeStruct((2, nx, ny, TILES) + tile, jnp.float32),
            jax.ShapeDtypeStruct((2 * nx, ny) + tile, jnp.float32),
        ),
        in_specs=[pl.BlockSpec(memory_space=pltpu.VMEM)] * 7,
        out_specs=[pl.BlockSpec(memory_space=pltpu.VMEM)] * 2,
        scratch_shapes=[
            buffer(ny, *tile),
            buffer(2 * nx, ny, *tile),
            buffer(*tile),
            buffer(ny - 1, *tile),
            buffer(2 * nx - 1, *tile),
            buffer(nz - 1, *tile),
            buffer(*tile),
            buffer(*tile),
            buffer(samples, sites, C, dtype=jnp.bfloat16),
            buffer(samples, sites, C),
            buffer(samples, NE, C, dtype=jnp.bfloat16),
            buffer(samples, NE, NE),
            buffer(samples, NE, NE, dtype=jnp.bfloat16),
            buffer(samples, sites, C, dtype=jnp.bfloat16),
            buffer(C, samples * NE, dtype=jnp.bfloat16),
            buffer(C, C),
            buffer(NE, NE),
            buffer(9 * C, C),
            buffer(C, NE),
            pltpu.SemaphoreType.DMA((copies,)),
            pltpu.SemaphoreType.DMA((copies,)),
        ],
        compiler_params=pltpu.CompilerParams(
            collective_id=0, has_side_effects=True, vmem_limit_bytes=48 * 2**20
        ),
    )(
        occupations.reshape(samples, 1, NE),
        occupations.reshape(samples, NE, 1),
        energy,
        inverse_tile,
        embed_weight,
        conv_weight,
        head_weight,
    )


def reduce_kernel(
    nx, ny, nz, parts_ref, chunk_ref, gathered_ref,
    from_core, sum_core, from_x, sum_x, from_y, sum_y, from_z, sum_z, got_z,
    block, block_y, block_k, send_sem, recv_sem,
):
    place = Place(nx, ny, nz)
    place.wait_peers(place.signal_peers())
    send = Sender(send_sem, recv_sem)
    order = [*range(1, nx), 0]
    other = 1 - place.c
    at_x = [lax.rem(place.x + d, nx) for d in order]
    copies = [send(parts_ref.at[other, i], from_core.at[i], place.core()) for i in at_x]
    sent = []
    for d, i, copy in zip(order, at_x, copies):
        copy.wait()
        sum_core[i] = parts_ref[place.c, i] + from_core[i]
        if d:
            sent.append(send(sum_core.at[i], from_x.at[d - 1], place.along_x(d)))
    wait_all(sent)
    sum_x[...] = total_of(sum_core[place.x], from_x, nx - 1)
    wait_all(
        [
            send(sum_x.at[lax.rem(place.y + d, ny)], from_y.at[d - 1], place.along_y(d))
            for d in range(1, ny)
        ]
    )
    sum_y[...] = jnp.zeros_like(sum_y)
    sum_y[0:TILES] = total_of(sum_x[place.y], from_y, ny - 1)
    wait_all(
        [
            send(sum_y.at[lax.rem(place.z + d, nz)], from_z.at[d - 1], place.along_z(d))
            for d in range(1, nz)
        ]
    )
    sum_z[...] = total_of(sum_y[place.z], from_z, nz - 1)
    copies = [send(sum_z, got_z.at[d], place.along_z(d)) for d in range(1, nz)]
    chunk_ref[place.z] = sum_z[...]
    wait_all(copies)
    for d in range(1, nz):
        chunk_ref[lax.rem(place.z - d + nz, nz)] = got_z[d]
    conv = chunk_ref[0:9]
    squares = jnp.sum(jnp.sum(conv * conv, axis=0), axis=0, keepdims=True)
    row = lax.broadcasted_iota(jnp.int32, (8, 128), 0)
    block[...] = jnp.where(row == 6, jnp.broadcast_to(squares, (8, 128)), chunk_ref[TILES - 1])
    copies = [send(block, block_y.at[d], place.along_y(d)) for d in range(1, ny)]
    block_y[0] = block[...]
    wait_all(copies)
    copies = [send(block_y, block_k.at[d], place.along_k(d)) for d in range(1, 2 * nx)]
    block_k[0] = block_y[...]
    wait_all(copies)
    spread(place, block_k, gathered_ref)


def reduce(nx, ny, nz, parts):
    tile = (8, 128)
    copies = nx + (nx - 1) + 2 * (ny - 1) + 2 * (nz - 1) + 2 * nx - 1

    def buffer(*lead):
        return pltpu.VMEM(lead + tile, jnp.float32)

    return pl.pallas_call(
        functools.partial(reduce_kernel, nx, ny, nz),
        name="reduce_parts",
        out_shape=(
            jax.ShapeDtypeStruct((nz,) + tile, jnp.float32),
            jax.ShapeDtypeStruct((2 * nx, ny) + tile, jnp.float32),
        ),
        in_specs=[pl.BlockSpec(memory_space=pltpu.VMEM)],
        out_specs=[pl.BlockSpec(memory_space=pltpu.VMEM)] * 2,
        scratch_shapes=[
            buffer(nx, ny, TILES),
            buffer(nx, ny, TILES),
            buffer(nx - 1, ny, TILES),
            buffer(ny, TILES),
            buffer(ny - 1, TILES),
            buffer(nz),
            buffer(nz - 1),
            buffer(),
            buffer(nz),
            buffer(),
            buffer(ny),
            buffer(2 * nx, ny),
            pltpu.SemaphoreType.DMA((copies,)),
            pltpu.SemaphoreType.DMA((copies,)),
        ],
        compiler_params=pltpu.CompilerParams(collective_id=1, has_side_effects=True),
    )(parts)


def in_order(nx, ny, gathered):
    split = gathered.reshape(nx, 2, ny, gathered.shape[-2], 128)
    return split.transpose(0, 2, 1, 3, 4).reshape(2 * nx * ny, gathered.shape[-2], 128)


def widen(rows):
    half = rows.shape[-2] // 2
    return jnp.concatenate([rows[..., :half, :], rows[..., half:, :]], axis=-1)


def rows_of(chunk, aligned, c):
    main = 8 * aligned
    edge = jnp.concatenate([chunk[2 * main : 2 * main + 4], chunk[2 * main + 4 : 2 * main + 8]], axis=1)
    if aligned == 0:
        return edge
    inner = jnp.concatenate([chunk[:main], chunk[main : 2 * main]], axis=1)
    after = jnp.concatenate([inner, edge], axis=0)
    before = jnp.concatenate([edge, inner], axis=0)
    return jnp.where(c == 0, after, before)


def per_device(
    nx,
    ny,
    nz,
    occupations,
    local_energy,
    embed_weight,
    conv_weight,
    head_weight,
    a_factor,
    g_factor,
    a_inverse,
    g_inverse,
):
    samples_all = occupations.shape[0] * 2 * nx * ny * nz
    inverse_tile = jnp.concatenate([a_inverse[:, :128], a_inverse[:, 128:]], axis=0)
    energy = jnp.broadcast_to(local_energy[:, None, None], local_energy.shape + (8, 128))
    embed_padded = jnp.pad(embed_weight, ((0, 128 - embed_weight.shape[0]), (0, 0)))
    parts, inverse_tiles = local_parts(
        nx, ny, nz, occupations, energy, inverse_tile, embed_padded, conv_weight, head_weight
    )
    chunk, gathered = reduce(nx, ny, nz, parts)
    chunk = chunk.reshape(nz * 8, 128)
    core = lax.rem(lax.axis_index("orb"), 2)
    conv_panel = rows_of(chunk[:72], 4, core)
    input_rows = rows_of(chunk[72:80], 0, core)
    blocks = in_order(nx, ny, gathered)
    head_grad = blocks[:, 0:4].reshape(C, NE)
    output_sum = blocks[:, 4:6].reshape(NE, NE)
    conv_norm = jnp.sum(blocks[:, 6])
    inverse_whole = widen(in_order(nx, ny, inverse_tiles)).reshape(C, C)
    left_applied = jnp.dot(inverse_whole, head_grad, precision=lax.Precision.HIGHEST)
    precond = jnp.dot(left_applied, g_inverse, precision=lax.Precision.HIGHEST)
    head_norm = jnp.sum(precond * head_grad)
    head_rows = C // (2 * nx * ny)
    precond_rows = lax.dynamic_slice_in_dim(
        precond, lax.axis_index("orb") * head_rows, head_rows, 0
    )
    head_update = -jnp.sqrt(C * NE / 4.0 / head_norm) * precond_rows
    conv_update = -jnp.sqrt(9 * C * C / 4.0 / conv_norm) * conv_panel
    new_a_factor = decay_rate * a_factor + (1.0 - decay_rate) * input_rows / (samples_all * NE)
    new_g_factor = decay_rate * g_factor + (1.0 - decay_rate) * output_sum / samples_all
    return (head_update, conv_update, new_a_factor, new_g_factor)


def solution(mesh):
    nz, orb = mesh.shape["walker"], mesh.shape["orb"]
    in_specs = (
        P(("walker", "orb"), None),
        P(("walker", "orb")),
        P(),
        P(),
        P(),
        P("orb", None),
        P(),
        P("orb", None),
        P(),
    )
    out_specs = (P("orb", None), P("orb", None), P("orb", None), P())
    return jax.shard_map(
        functools.partial(per_device, X_CHIPS, orb // (2 * X_CHIPS), nz),
        mesh=mesh,
        in_specs=in_specs,
        out_specs=out_specs,
        check_vma=False,
    )
```

```python
import functools
import math

import jax
import jax.numpy as jnp
from jax import lax
from jax.experimental import pallas as pl
from jax.experimental.pallas import tpu as pltpu
from jax.sharding import PartitionSpec as P

L = 16
C = 256
NS_STEPS = 3
NE = 128
X_CHIPS = 4
TILES = 11
HALF = 6

decay_rate = 0.8
MESH = pl.DeviceIdType.MESH


class Place:
    def __init__(self, nx, ny, nz):
        self.nx, self.ny, self.nz = nx, ny, nz
        self.z = lax.axis_index("walker")
        self.orb = lax.axis_index("orb")
        self.c = lax.rem(self.orb, 2)
        self.y = lax.rem(lax.div(self.orb, 2), ny)
        self.x = lax.div(self.orb, 2 * ny)
        self.k = self.x * 2 + self.c

    def at(self, x, y, c):
        return (self.z, (x * self.ny + y) * 2 + c)

    def core(self):
        return self.at(self.x, self.y, 1 - self.c)

    def along_x(self, d):
        return self.at(lax.rem(self.x + d, self.nx), self.y, self.c)

    def along_y(self, d):
        return self.at(self.x, lax.rem(self.y + d, self.ny), self.c)

    def along_k(self, d):
        k = lax.rem(self.k + d, 2 * self.nx)
        return self.at(lax.div(k, 2), self.y, lax.rem(k, 2))

    def along_z(self, d):
        return (lax.rem(self.z + d, self.nz), self.orb)

    def signal_peers(self):
        barrier = pltpu.get_barrier_semaphore()
        peers = [self.along_y(d) for d in range(1, self.ny)]
        peers += [self.along_k(d) for d in range(1, 2 * self.nx)]
        peers += [self.along_z(d) for d in range(1, self.nz)]
        for peer in peers:
            pl.semaphore_signal(barrier, inc=1, device_id=peer, device_id_type=MESH)
        return len(peers)

    def wait_peers(self, count):
        pl.semaphore_wait(pltpu.get_barrier_semaphore(), count)


class Sender:
    def __init__(self, send_sem, recv_sem):
        self.send_sem, self.recv_sem, self.used = send_sem, recv_sem, 0

    def __call__(self, source, target, device):
        copy = pltpu.make_async_remote_copy(
            src_ref=source,
            dst_ref=target,
            send_sem=self.send_sem.at[self.used],
            recv_sem=self.recv_sem.at[self.used],
            device_id=device,
            device_id_type=MESH,
        )
        copy.start()
        self.used += 1
        return copy


def wait_all(copies):
    for copy in copies:
        copy.wait()


def total_of(first, ref, count):
    total = first
    for i in range(count):
        total = total + ref[i]
    return total


def spread(place, slots_ref, out_ref):
    for i in range(2 * place.nx):
        k = lax.rem(place.k - i + 2 * place.nx, 2 * place.nx)
        for j in range(place.ny):
            y = lax.rem(place.y - j + place.ny, place.ny)
            out_ref[k, y] = slots_ref[i, j]


def site_shift_y(field, b):
    if b == 0:
        return field
    y = lax.broadcasted_iota(jnp.int32, field.shape, 0) & (L - 1)
    sites = field.shape[0]
    if b == 1:
        edge, inside = pltpu.roll(field, L - 1, 0), pltpu.roll(field, sites - 1, 0)
        return jnp.where(y == L - 1, edge, inside)
    edge, inside = pltpu.roll(field, sites - L + 1, 0), pltpu.roll(field, 1, 0)
    return jnp.where(y == 0, edge, inside)


def site_shift_x(field, a):
    if a == 0:
        return field
    cut = L if a == 1 else field.shape[0] - L
    return jnp.concatenate([field[cut:], field[:cut]], axis=0)


def site_patches(field, sign):
    by_y = {b: site_shift_y(field, sign * b).astype(jnp.bfloat16) for b in (-1, 0, 1)}
    return jnp.concatenate(
        [site_shift_x(by_y[b], sign * a) for a in (-1, 0, 1) for b in (-1, 0, 1)], axis=1
    )


def multiply(left, right):
    return jnp.dot(
        left.astype(jnp.bfloat16), right.astype(jnp.bfloat16), preferred_element_type=jnp.float32
    )


def electrons_by_site(occ_ref, b):
    sites = lax.broadcasted_iota(jnp.int32, (L * L, NE), 0)
    return (sites == occ_ref[b : b + 1, :]).astype(jnp.float32)


def forward(b, occ_ref, embed_ref, conv_w_ref, head_w_ref,
            embedded_ref, slope_ref, rows_ref, log_ref):
    by_site = electrons_by_site(occ_ref, b)
    electron = lax.broadcasted_iota(jnp.int32, (NE, 128), 0)
    lane = lax.broadcasted_iota(jnp.int32, (NE, 128), 1)
    down = (electron >= NE // 2).astype(jnp.int32)
    spin = ((lane & 1) == down).astype(jnp.float32)
    counts = multiply(by_site, spin)
    tap_of_lane = lax.broadcasted_iota(jnp.int32, counts.shape, 1) >> 1
    near = jnp.zeros_like(counts)
    for j in (-1, 0, 1):
        at_y = site_shift_y(counts, j)
        for i in (-1, 0, 1):
            tap = (i + 1) * 3 + j + 1
            near = jnp.where(tap_of_lane == tap, site_shift_x(at_y, i), near)
    embedded = jnp.tanh(multiply(near[:, : embed_ref.shape[0]], embed_ref[...])).astype(jnp.bfloat16)
    embedded_ref[b] = embedded
    wide = embedded.astype(jnp.float32)
    squash = jnp.tanh(multiply(site_patches(wide, 1), conv_w_ref[...]))
    slope_ref[b] = 1.0 - squash * squash
    hidden = (wide + squash).astype(jnp.bfloat16)
    rows = multiply(by_site.T, hidden).astype(jnp.bfloat16)
    rows_ref[b] = rows
    orbital_tanh = jnp.tanh(multiply(rows, head_w_ref[...]))
    shift = (0.35 / math.sqrt(NE)) * orbital_tanh
    row = lax.broadcasted_iota(jnp.int32, (NE, NE), 0)
    column = lax.broadcasted_iota(jnp.int32, (NE, NE), 1)
    identity = (row == column).astype(jnp.float32)
    second = multiply(shift, shift)
    inverse_est = identity - shift + second - multiply(shift, second)
    inverse_est = inverse_est + multiply(inverse_est, multiply(second, second))
    log_ref[b] = (1.0 - orbital_tanh * orbital_tanh) * inverse_est.T


def backward(b, occ_ref, head_w_ref, slope_ref, log_ref, cot_ref, pre_ref):
    cotangent = ((0.35 / math.sqrt(NE)) * log_ref[b]).astype(jnp.bfloat16)
    cot_ref[b] = cotangent
    row_grads = lax.dot_general(
        cotangent, head_w_ref[...], (((1,), (1,)), ((), ())), preferred_element_type=jnp.float32
    ).astype(jnp.bfloat16)
    hidden_grad = multiply(electrons_by_site(occ_ref, b), row_grads)
    pre_ref[b] = (hidden_grad * slope_ref[b]).astype(jnp.bfloat16)


def grams(samples, rows_ref, log_ref, rows_t_ref, input_ref, output_ref):
    rows = rows_ref[...].reshape(samples * NE, C)
    rows_t = rows.astype(jnp.float32).T.astype(jnp.bfloat16)
    rows_t_ref[...] = rows_t
    input_ref[...] = multiply(rows_t, rows)
    logs = log_ref[...].reshape(samples * NE, NE)
    output_ref[...] = jnp.dot(
        logs.T, logs, precision=lax.Precision.HIGHEST, preferred_element_type=jnp.float32
    )


def weighted_sums(samples, weight_of, embedded_ref, pre_ref, rows_t_ref, cot_ref, conv_ref, head_ref):
    for b in range(samples):
        weight = weight_of(b)
        wide = jnp.concatenate([weight, weight], axis=1)
        embedded_t = embedded_ref[b].astype(jnp.float32).T
        terms = multiply(embedded_t, site_patches(pre_ref[b].astype(jnp.float32), -1))
        head = weight * multiply(rows_t_ref[:, b * NE : (b + 1) * NE], cot_ref[b])
        head_ref[...] = head if b == 0 else head_ref[...] + head
        for tap in range(9):
            rows = slice(tap * C, (tap + 1) * C)
            term = wide * terms[:, rows]
            conv_ref[rows, :] = term if b == 0 else conv_ref[rows, :] + term


def lay_out(nx, ny, conv_ref, input_ref, head_ref, output_ref, parts_ref):
    row = lax.broadcasted_iota(jnp.int32, (8, 128), 0)

    def halves(first, second, c):
        if c == 0:
            return jnp.where(row < 4, first, pltpu.roll(second, 4, 0))
        return jnp.where(row < 4, pltpu.roll(first, 4, 0), second)

    for pair in range(nx * ny):
        x, y = pair // ny, pair % ny
        for c in range(2):
            top = 72 * pair + 40 * c
            for half in range(2):
                lanes = slice(128 * half, 128 * half + 128)
                for i in range(4):
                    tile = conv_ref[top + 8 * i : top + 8 * i + 8, lanes]
                    parts_ref[c, x, y, 4 * half + i] = tile
            middle = slice(72 * pair + 32, 72 * pair + 40)
            parts_ref[c, x, y, 8] = halves(conv_ref[middle, :128], conv_ref[middle, 128:], c)
            eight = slice(8 * pair, 8 * pair + 8)
            parts_ref[c, x, y, 9] = halves(input_ref[eight, :128], input_ref[eight, 128:], c)
            place = 4 * (pair % 2) + 2 * c
            output = output_ref[8 * (pair // 2) : 8 * (pair // 2) + 8, :]
            output = pltpu.roll(output, (4 - place) % 8, 0) if place != 4 else output
            head = head_ref[eight, :] if c == 0 else pltpu.roll(head_ref[eight, :], 4, 0)
            parts_ref[c, x, y, 10] = jnp.where(row < 4, head, output)


def row_index():
    return lax.broadcasted_iota(jnp.int32, (8, 128), 0)


def inverse_from(nx, ny, gathered_ref, inverse_ref):
    row = row_index()
    for pair in range(nx * ny):
        x, y = pair // ny, pair % ny
        first, second = gathered_ref[2 * x, y], gathered_ref[2 * x + 1, y]
        eight = slice(8 * pair, 8 * pair + 8)
        inverse_ref[eight, :128] = jnp.where(row < 4, first, pltpu.roll(second, 4, 0))
        inverse_ref[eight, 128:] = jnp.where(row < 4, pltpu.roll(first, 4, 0), second)


def head_from(nx, ny, gathered_ref, head_ref, output_ref):
    row = row_index()
    squares = jnp.zeros((8, 128), jnp.float32)
    for pair in range(0, nx * ny, 2):
        tiles = []
        for p in (pair, pair + 1):
            x, y = p // ny, p % ny
            first, second = gathered_ref[2 * x, y], gathered_ref[2 * x + 1, y]
            head_ref[8 * p : 8 * p + 8, :] = jnp.where(row < 4, first, pltpu.roll(second, 4, 0))
            squares = squares + (first + second)
            tiles += [first, second]
        upper = jnp.where(row < 2, pltpu.roll(tiles[0], 4, 0), pltpu.roll(tiles[1], 6, 0))
        lower = jnp.where(row < 6, tiles[2], pltpu.roll(tiles[3], 2, 0))
        output_ref[4 * pair : 4 * pair + 8, :] = jnp.where(row < 4, upper, lower)
    return jnp.sum(squares[6:7], axis=1, keepdims=True)


def exchange(
    place, send, parts_ref, chunk_ref, gathered_ref,
    from_core, sum_core, relay_up, relay_down, from_x, sum_x, from_y, sum_y, from_z, sum_z, got_z,
    block, block_y, block_k,
):
    nx, ny, nz = place.nx, place.ny, place.nz
    order = sorted(range(1, ny), key=lambda d: -min(d, ny - d)) + [0]
    at_x = [lax.rem(place.x + d, nx) for d in range(nx)]
    at_y = [lax.rem(place.y + d, ny) for d in range(ny)]
    low, high = pl.ds(0, HALF), pl.ds(HALF, TILES - HALF)
    core, relays, across, along = {}, {}, {}, []
    for d in order:
        source = parts_ref.at[1 - place.c, :, at_y[d]]
        core[d] = send(source, from_core.at[:, at_y[d]], place.core())
    for d in order:
        core[d].wait()
        sum_core[:, at_y[d]] = parts_ref[place.c, :, at_y[d]] + from_core[:, at_y[d]]
        relays[d] = [
            send(sum_core.at[at_x[2], at_y[d], low], relay_up.at[d], place.along_x(1)),
            send(sum_core.at[at_x[2], at_y[d], high], relay_down.at[d], place.along_x(nx - 1)),
        ]
    for d in order:
        wait_all(relays[d])
        sum_core[at_x[1], at_y[d], low] = sum_core[at_x[1], at_y[d], low] + relay_up[d]
        sum_core[at_x[3], at_y[d], high] = sum_core[at_x[3], at_y[d], high] + relay_down[d]
        across[d] = [
            send(sum_core.at[at_x[1], at_y[d]], from_x.at[0, d], place.along_x(1)),
            send(sum_core.at[at_x[3], at_y[d]], from_x.at[1, d], place.along_x(nx - 1)),
        ]
    for d in order:
        wait_all(across[d])
        sum_x[d] = sum_core[place.x, at_y[d]] + (from_x[0, d] + from_x[1, d])
        if d:
            along.append(send(sum_x.at[d], from_y.at[d - 1], place.along_y(d)))
    wait_all(along)
    sum_y[TILES:nz] = jnp.zeros((nz - TILES, 8, 128), jnp.float32)
    sum_y[0:TILES] = total_of(sum_x[0], from_y, ny - 1)
    wait_all(
        [
            send(sum_y.at[lax.rem(place.z + d, nz)], from_z.at[d - 1], place.along_z(d))
            for d in range(1, nz)
        ]
    )
    sum_z[...] = total_of(sum_y[place.z], from_z, nz - 1)
    copies = [send(sum_z, got_z.at[d], place.along_z(d)) for d in range(1, nz)]
    chunk_ref[place.z] = sum_z[...]
    wait_all(copies)
    for d in range(1, nz):
        chunk_ref[lax.rem(place.z - d + nz, nz)] = got_z[d]
    conv = chunk_ref[0:9]
    squares = jnp.sum(jnp.sum(conv * conv, axis=0), axis=0, keepdims=True)
    block[...] = jnp.where(
        row_index() == 6, jnp.broadcast_to(squares, (8, 128)), chunk_ref[TILES - 1]
    )
    copies = [send(block, block_y.at[d], place.along_y(d)) for d in range(1, ny)]
    block_y[0] = block[...]
    wait_all(copies)
    copies = [send(block_y, block_k.at[d], place.along_k(d)) for d in range(1, 2 * nx)]
    block_k[0] = block_y[...]
    wait_all(copies)
    spread(place, block_k, gathered_ref)


def dot_highest(left, right):
    return jnp.dot(
        left, right, precision=lax.Precision.HIGHEST, preferred_element_type=jnp.float32
    )


def updates(
    place, samples_all, chunk_ref, gathered_ref, a_factor_ref, g_factor_ref, g_inverse_ref,
    inverse_ref, head_ref, output_ref, precond_ref,
    head_update_ref, conv_update_ref, new_a_ref, new_g_ref,
):
    conv_norm = head_from(place.nx, place.ny, gathered_ref, head_ref, output_ref)
    head_grad = head_ref[...]
    precond = dot_highest(dot_highest(inverse_ref[...], head_grad), g_inverse_ref[...])
    precond_ref[...] = precond
    head_norm = jnp.sum(
        jnp.sum(precond * head_grad, axis=0, keepdims=True), axis=1, keepdims=True
    )
    head_scale = -jnp.sqrt(C * NE / 4.0 / head_norm)
    conv_scale = -jnp.sqrt(9 * C * C / 4.0 / conv_norm)
    pair = pl.multiple_of(lax.div(place.orb, 2) * 8, 8)
    eight = head_scale * precond_ref[pl.ds(pair, 8), :]
    head_update_ref[...] = jnp.where(place.c == 0, eight, pltpu.roll(eight, 4, 0))[0:4]
    keep = 1.0 - decay_rate
    for half in range(2):
        lanes = slice(128 * half, 128 * half + 128)
        rows = slice(4 * half, 4 * half + 4)
        input_rows = chunk_ref[9][rows]
        new_a_ref[:, lanes] = (
            decay_rate * a_factor_ref[:, lanes] + keep * input_rows / (samples_all * NE)
        )
        inner = conv_scale * chunk_ref[4 * half : 4 * half + 4].reshape(32, 128)
        edge = conv_scale * chunk_ref[8][rows]

        @pl.when(place.c == 0)
        def _(lanes=lanes, inner=inner, edge=edge):
            conv_update_ref[0:32, lanes] = inner
            conv_update_ref[32:36, lanes] = edge

        @pl.when(place.c == 1)
        def _(lanes=lanes, inner=inner, edge=edge):
            conv_update_ref[0:4, lanes] = edge
            conv_update_ref[4:36, lanes] = inner

    new_g_ref[...] = decay_rate * g_factor_ref[...] + keep * output_ref[...] / samples_all


def step_kernel(
    nx, ny, nz, samples,
    occ_in, energy_in, a_inverse_in, embed_in, conv_w_in, head_w_in,
    a_factor_in, g_factor_in, g_inverse_in,
    head_update_ref, conv_update_ref, new_a_ref, new_g_ref,
    occ_ref, energy_ref, a_inverse_ref, embed_ref, conv_w_ref, head_w_ref,
    a_factor_ref, g_factor_ref, g_inverse_ref,
    rows_own, rows_y, rows_k, energy_own, energy_y, energy_k, energy_z, part_k, part_z,
    embedded_ref, slope_ref, rows_ref, log_ref, cot_ref, pre_ref, rows_t_ref,
    input_ref, output_ref, conv_ref, head_ref, parts_ref, gathered_ref, inverse_ref, precond_ref,
    chunk_ref, *rest,
):
    *buffers, load_sem, send_sem, recv_sem = rest
    place = Place(nx, ny, nz)
    peers = place.signal_peers()
    loads = [
        pltpu.make_async_copy(source, target, load_sem.at[i])
        for i, (source, target) in enumerate(
            [
                (occ_in, occ_ref),
                (energy_in, energy_ref),
                (a_inverse_in, a_inverse_ref),
                (embed_in, embed_ref),
                (conv_w_in, conv_w_ref),
                (head_w_in, head_w_ref),
                (a_factor_in, a_factor_ref),
                (g_factor_in, g_factor_ref),
                (g_inverse_in, g_inverse_ref),
            ]
        )
    ]
    for load in loads:
        load.start()
    send = Sender(send_sem, recv_sem)

    def energy_of(b):
        return jnp.broadcast_to(energy_ref[0:1, b : b + 1], (8, 128))

    def sample(b):
        forward(b, occ_ref, embed_ref, conv_w_ref, head_w_ref,
                embedded_ref, slope_ref, rows_ref, log_ref)

    wait_all(loads[:6])
    energy_own[...] = sum((energy_of(b) for b in range(1, samples)), energy_of(0))
    rows_own[0:4, :] = a_inverse_ref[:, :128]
    rows_own[4:8, :] = a_inverse_ref[:, 128:]
    sample(0)
    place.wait_peers(peers)
    energies = [send(energy_own, energy_y.at[d - 1], place.along_y(d)) for d in range(1, ny)]
    rows = [send(rows_own, rows_y.at[d], place.along_y(d)) for d in range(1, ny)]
    rows_y[0] = rows_own[...]
    sample(1)
    wait_all(energies)
    part_k[...] = total_of(energy_own[...], energy_y, ny - 1)
    energies = [send(part_k, energy_k.at[d - 1], place.along_k(d)) for d in range(1, 2 * nx)]
    wait_all(rows)
    rows = [send(rows_y, rows_k.at[d], place.along_k(d)) for d in range(1, 2 * nx)]
    rows_k[0] = rows_y[...]
    for b in range(2, samples):
        sample(b)
    wait_all(energies)
    part_z[...] = total_of(part_k[...], energy_k, 2 * nx - 1)
    energies = [send(part_z, energy_z.at[d - 1], place.along_z(d)) for d in range(1, nz)]
    for b in range(samples):
        backward(b, occ_ref, head_w_ref, slope_ref, log_ref, cot_ref, pre_ref)
    grams(samples, rows_ref, log_ref, rows_t_ref, input_ref, output_ref)
    wait_all(rows)
    spread(place, rows_k, gathered_ref)
    inverse_from(nx, ny, gathered_ref, inverse_ref)
    wait_all(energies)
    total = total_of(part_z[...], energy_z, nz - 1)[0:1]
    samples_all = samples * 2 * nx * ny * nz
    mean_energy = total / samples_all
    weighted_sums(
        samples,
        lambda b: (energy_of(b)[0:1] - mean_energy) / samples_all,
        embedded_ref, pre_ref, rows_t_ref, cot_ref, conv_ref, head_ref,
    )
    lay_out(nx, ny, conv_ref, input_ref, head_ref, output_ref, parts_ref)
    wait_all(loads[6:])
    exchange(place, send, parts_ref, chunk_ref, gathered_ref, *buffers)
    updates(
        place, samples_all, chunk_ref, gathered_ref, a_factor_ref, g_factor_ref, g_inverse_ref,
        inverse_ref, head_ref, output_ref, precond_ref,
        head_update_ref, conv_update_ref, new_a_ref, new_g_ref,
    )


def per_device(
    nx,
    ny,
    nz,
    occupations,
    local_energy,
    embed_weight,
    conv_weight,
    head_weight,
    a_factor,
    g_factor,
    a_inverse,
    g_inverse,
):
    samples = occupations.shape[0]
    sites = L * L
    orb = 2 * nx * ny
    copies = 2 * (ny - 1) + 2 * (2 * nx - 1) + nz - 1
    copies += 5 * ny + 2 * (ny - 1) + 2 * (nz - 1) + 2 * nx - 1

    inputs = (
        occupations,
        local_energy.reshape(1, samples),
        a_inverse,
        embed_weight,
        conv_weight,
        head_weight,
        a_factor,
        g_factor,
        g_inverse,
    )

    def buffer(*shape, dtype=jnp.float32):
        return pltpu.VMEM(shape, dtype)

    def tiles(*lead):
        return pltpu.VMEM(lead + (8, 128), jnp.float32)

    return pl.pallas_call(
        functools.partial(step_kernel, nx, ny, nz, samples),
        name="natural_step",
        out_shape=(
            jax.ShapeDtypeStruct((C // orb, NE), jnp.float32),
            jax.ShapeDtypeStruct((9 * C // orb, C), jnp.float32),
            jax.ShapeDtypeStruct((C // orb, C), jnp.float32),
            jax.ShapeDtypeStruct((NE, NE), jnp.float32),
        ),
        in_specs=[pl.BlockSpec(memory_space=pl.ANY)] * 9,
        out_specs=[pl.BlockSpec(memory_space=pltpu.VMEM)] * 4,
        scratch_shapes=[pltpu.VMEM(a.shape, a.dtype) for a in inputs]
        + [
            tiles(),
            tiles(ny),
            tiles(2 * nx, ny),
            tiles(),
            tiles(ny - 1),
            tiles(2 * nx - 1),
            tiles(nz - 1),
            tiles(),
            tiles(),
            buffer(samples, sites, C, dtype=jnp.bfloat16),
            buffer(samples, sites, C),
            buffer(samples, NE, C, dtype=jnp.bfloat16),
            buffer(samples, NE, NE),
            buffer(samples, NE, NE, dtype=jnp.bfloat16),
            buffer(samples, sites, C, dtype=jnp.bfloat16),
            buffer(C, samples * NE, dtype=jnp.bfloat16),
            buffer(C, C),
            buffer(NE, NE),
            buffer(9 * C, C),
            buffer(C, NE),
            tiles(2, nx, ny, TILES),
            tiles(2 * nx, ny),
            buffer(C, C),
            buffer(C, NE),
            tiles(nz),
            tiles(nx, ny, TILES),
            tiles(nx, ny, TILES),
            tiles(ny, HALF),
            tiles(ny, TILES - HALF),
            tiles(2, ny, TILES),
            tiles(ny, TILES),
            tiles(ny - 1, TILES),
            tiles(nz),
            tiles(nz - 1),
            tiles(),
            tiles(nz),
            tiles(),
            tiles(ny),
            tiles(2 * nx, ny),
            pltpu.SemaphoreType.DMA((len(inputs),)),
            pltpu.SemaphoreType.DMA((copies,)),
            pltpu.SemaphoreType.DMA((copies,)),
        ],
        compiler_params=pltpu.CompilerParams(collective_id=0, has_side_effects=True),
    )(*inputs)


def solution(mesh):
    nz, orb = mesh.shape["walker"], mesh.shape["orb"]
    in_specs = (
        P(("walker", "orb"), None),
        P(("walker", "orb")),
        P(),
        P(),
        P(),
        P("orb", None),
        P(),
        P("orb", None),
        P(),
    )
    out_specs = (P("orb", None), P("orb", None), P("orb", None), P())
    return jax.shard_map(
        functools.partial(per_device, X_CHIPS, orb // (2 * X_CHIPS), nz),
        mesh=mesh,
        in_specs=in_specs,
        out_specs=out_specs,
        check_vma=False,
    )
```

```python
import functools
import math

import jax
import jax.numpy as jnp
from jax import lax
from jax.experimental import pallas as pl
from jax.experimental.pallas import tpu as pltpu
from jax.sharding import PartitionSpec as P

L = 16
C = 256
NS_STEPS = 3
NE = 128
X_CHIPS = 4
TILES = 11
HALF = 6

decay_rate = 0.8
MESH = pl.DeviceIdType.MESH


class Place:
    def __init__(self, nx, ny, nz):
        self.nx, self.ny, self.nz = nx, ny, nz
        self.z = lax.axis_index("walker")
        self.orb = lax.axis_index("orb")
        self.c = lax.rem(self.orb, 2)
        self.y = lax.rem(lax.div(self.orb, 2), ny)
        self.x = lax.div(self.orb, 2 * ny)
        self.k = self.x * 2 + self.c

    def at(self, x, y, c):
        return (self.z, (x * self.ny + y) * 2 + c)

    def core(self):
        return self.at(self.x, self.y, 1 - self.c)

    def along_x(self, d):
        return self.at(lax.rem(self.x + d, self.nx), self.y, self.c)

    def along_y(self, d):
        return self.at(self.x, lax.rem(self.y + d, self.ny), self.c)

    def along_k(self, d):
        k = lax.rem(self.k + d, 2 * self.nx)
        return self.at(lax.div(k, 2), self.y, lax.rem(k, 2))

    def along_z(self, d):
        return (lax.rem(self.z + d, self.nz), self.orb)

    def signal_peers(self):
        barrier = pltpu.get_barrier_semaphore()
        peers = [self.along_y(d) for d in range(1, self.ny)]
        peers += [self.along_k(d) for d in range(1, 2 * self.nx)]
        peers += [self.along_z(d) for d in range(1, self.nz)]
        for peer in peers:
            pl.semaphore_signal(barrier, inc=1, device_id=peer, device_id_type=MESH)
        return len(peers)

    def wait_peers(self, count):
        pl.semaphore_wait(pltpu.get_barrier_semaphore(), count)


class Sender:
    def __init__(self, send_sem, recv_sem):
        self.send_sem, self.recv_sem, self.used = send_sem, recv_sem, 0

    def __call__(self, source, target, device):
        copy = pltpu.make_async_remote_copy(
            src_ref=source,
            dst_ref=target,
            send_sem=self.send_sem.at[self.used],
            recv_sem=self.recv_sem.at[self.used],
            device_id=device,
            device_id_type=MESH,
        )
        copy.start()
        self.used += 1
        return copy


def wait_all(copies):
    for copy in copies:
        copy.wait()


def total_of(first, ref, count):
    total = first
    for i in range(count):
        total = total + ref[i]
    return total


def spread(place, slots_ref, out_ref):
    for i in range(2 * place.nx):
        k = lax.rem(place.k - i + 2 * place.nx, 2 * place.nx)
        for j in range(place.ny):
            y = lax.rem(place.y - j + place.ny, place.ny)
            out_ref[k, y] = slots_ref[i, j]


def site_shift_y(field, b):
    if b == 0:
        return field
    y = lax.broadcasted_iota(jnp.int32, field.shape, 0) & (L - 1)
    sites = field.shape[0]
    if b == 1:
        edge, inside = pltpu.roll(field, L - 1, 0), pltpu.roll(field, sites - 1, 0)
        return jnp.where(y == L - 1, edge, inside)
    edge, inside = pltpu.roll(field, sites - L + 1, 0), pltpu.roll(field, 1, 0)
    return jnp.where(y == 0, edge, inside)


def site_shift_x(field, a):
    if a == 0:
        return field
    cut = L if a == 1 else field.shape[0] - L
    return jnp.concatenate([field[cut:], field[:cut]], axis=0)


def site_patches(field, sign):
    by_y = {b: site_shift_y(field, sign * b).astype(jnp.bfloat16) for b in (-1, 0, 1)}
    return jnp.concatenate(
        [site_shift_x(by_y[b], sign * a) for a in (-1, 0, 1) for b in (-1, 0, 1)], axis=1
    )


def multiply(left, right):
    return jnp.dot(
        left.astype(jnp.bfloat16), right.astype(jnp.bfloat16), preferred_element_type=jnp.float32
    )


def electrons_by_site(occ_ref, b):
    sites = lax.broadcasted_iota(jnp.int32, (L * L, NE), 0)
    return (sites == occ_ref[b : b + 1, :]).astype(jnp.float32)


def forward(b, occ_ref, embed_ref, conv_w_ref, head_w_ref,
            embedded_ref, slope_ref, rows_ref, log_ref):
    by_site = electrons_by_site(occ_ref, b)
    electron = lax.broadcasted_iota(jnp.int32, (NE, 128), 0)
    lane = lax.broadcasted_iota(jnp.int32, (NE, 128), 1)
    down = (electron >= NE // 2).astype(jnp.int32)
    spin = ((lane & 1) == down).astype(jnp.float32)
    counts = multiply(by_site, spin)
    tap_of_lane = lax.broadcasted_iota(jnp.int32, counts.shape, 1) >> 1
    near = jnp.zeros_like(counts)
    for j in (-1, 0, 1):
        at_y = site_shift_y(counts, j)
        for i in (-1, 0, 1):
            tap = (i + 1) * 3 + j + 1
            near = jnp.where(tap_of_lane == tap, site_shift_x(at_y, i), near)
    embedded = jnp.tanh(multiply(near[:, : embed_ref.shape[0]], embed_ref[...])).astype(jnp.bfloat16)
    embedded_ref[b] = embedded
    wide = embedded.astype(jnp.float32)
    squash = jnp.tanh(multiply(site_patches(wide, 1), conv_w_ref[...]))
    slope_ref[b] = 1.0 - squash * squash
    hidden = (wide + squash).astype(jnp.bfloat16)
    rows = multiply(by_site.T, hidden).astype(jnp.bfloat16)
    rows_ref[b] = rows
    orbital_tanh = jnp.tanh(multiply(rows, head_w_ref[...]))
    shift = (0.35 / math.sqrt(NE)) * orbital_tanh
    row = lax.broadcasted_iota(jnp.int32, (NE, NE), 0)
    column = lax.broadcasted_iota(jnp.int32, (NE, NE), 1)
    identity = (row == column).astype(jnp.float32)
    second = multiply(shift, shift)
    inverse_est = identity - shift + second - multiply(shift, second)
    inverse_est = inverse_est + multiply(inverse_est, multiply(second, second))
    log_ref[b] = (1.0 - orbital_tanh * orbital_tanh) * inverse_est.T


def backward(b, occ_ref, head_w_ref, slope_ref, log_ref, cot_ref, pre_ref):
    cotangent = ((0.35 / math.sqrt(NE)) * log_ref[b]).astype(jnp.bfloat16)
    cot_ref[b] = cotangent
    row_grads = lax.dot_general(
        cotangent, head_w_ref[...], (((1,), (1,)), ((), ())), preferred_element_type=jnp.float32
    ).astype(jnp.bfloat16)
    hidden_grad = multiply(electrons_by_site(occ_ref, b), row_grads)
    pre_ref[b] = (hidden_grad * slope_ref[b]).astype(jnp.bfloat16)


def grams(samples, rows_ref, log_ref, rows_t_ref, input_ref, output_ref):
    rows = rows_ref[...].reshape(samples * NE, C)
    rows_t = rows.astype(jnp.float32).T.astype(jnp.bfloat16)
    rows_t_ref[...] = rows_t
    input_ref[...] = multiply(rows_t, rows)
    logs = log_ref[...].reshape(samples * NE, NE)
    output_ref[...] = jnp.dot(
        logs.T, logs, precision=lax.Precision.HIGHEST, preferred_element_type=jnp.float32
    )


def weighted_sums(samples, weight_of, embedded_ref, pre_ref, rows_t_ref, cot_ref, conv_ref, head_ref):
    for b in range(samples):
        weight = weight_of(b)
        wide = jnp.concatenate([weight, weight], axis=1)
        embedded_t = embedded_ref[b].astype(jnp.float32).T
        terms = multiply(embedded_t, site_patches(pre_ref[b].astype(jnp.float32), -1))
        head = weight * multiply(rows_t_ref[:, b * NE : (b + 1) * NE], cot_ref[b])
        head_ref[...] = head if b == 0 else head_ref[...] + head
        for tap in range(9):
            rows = slice(tap * C, (tap + 1) * C)
            term = wide * terms[:, rows]
            conv_ref[rows, :] = term if b == 0 else conv_ref[rows, :] + term


def lay_out(nx, ny, conv_ref, input_ref, head_ref, output_ref, parts_ref):
    row = lax.broadcasted_iota(jnp.int32, (8, 128), 0)

    def halves(first, second, c):
        if c == 0:
            return jnp.where(row < 4, first, pltpu.roll(second, 4, 0))
        return jnp.where(row < 4, pltpu.roll(first, 4, 0), second)

    for pair in range(nx * ny):
        x, y = pair // ny, pair % ny
        for c in range(2):
            top = 72 * pair + 40 * c
            for half in range(2):
                lanes = slice(128 * half, 128 * half + 128)
                for i in range(4):
                    tile = conv_ref[top + 8 * i : top + 8 * i + 8, lanes]
                    parts_ref[c, x, y, 4 * half + i] = tile
            middle = slice(72 * pair + 32, 72 * pair + 40)
            parts_ref[c, x, y, 8] = halves(conv_ref[middle, :128], conv_ref[middle, 128:], c)
            eight = slice(8 * pair, 8 * pair + 8)
            parts_ref[c, x, y, 9] = halves(input_ref[eight, :128], input_ref[eight, 128:], c)
            place = 4 * (pair % 2) + 2 * c
            output = output_ref[8 * (pair // 2) : 8 * (pair // 2) + 8, :]
            output = pltpu.roll(output, (4 - place) % 8, 0) if place != 4 else output
            head = head_ref[eight, :] if c == 0 else pltpu.roll(head_ref[eight, :], 4, 0)
            parts_ref[c, x, y, 10] = jnp.where(row < 4, head, output)


def row_index():
    return lax.broadcasted_iota(jnp.int32, (8, 128), 0)


def inverse_from(nx, ny, gathered_ref, inverse_ref):
    row = row_index()
    for pair in range(nx * ny):
        x, y = pair // ny, pair % ny
        first, second = gathered_ref[2 * x, y], gathered_ref[2 * x + 1, y]
        eight = slice(8 * pair, 8 * pair + 8)
        inverse_ref[eight, :128] = jnp.where(row < 4, first, pltpu.roll(second, 4, 0))
        inverse_ref[eight, 128:] = jnp.where(row < 4, pltpu.roll(first, 4, 0), second)


def head_from(nx, ny, gathered_ref, head_ref, output_ref):
    row = row_index()
    for pair in range(0, nx * ny, 2):
        tiles = []
        for p in (pair, pair + 1):
            x, y = p // ny, p % ny
            first, second = gathered_ref[2 * x, y], gathered_ref[2 * x + 1, y]
            head_ref[8 * p : 8 * p + 8, :] = jnp.where(row < 4, first, pltpu.roll(second, 4, 0))
            tiles += [first, second]
        upper = jnp.where(row < 2, pltpu.roll(tiles[0], 4, 0), pltpu.roll(tiles[1], 6, 0))
        lower = jnp.where(row < 6, tiles[2], pltpu.roll(tiles[3], 2, 0))
        output_ref[4 * pair : 4 * pair + 8, :] = jnp.where(row < 4, upper, lower)


def exchange(
    place, send, parts_ref, chunk_ref, gathered_ref,
    from_core, sum_core, relay_up, relay_down, from_x, sum_x, from_y, sum_y, from_z, sum_z, got_z,
    head_z, block, block_y, block_k, square, square_y, part_square, square_k,
):
    nx, ny, nz = place.nx, place.ny, place.nz
    order = sorted(range(1, ny), key=lambda d: -min(d, ny - d)) + [0]
    at_x = [lax.rem(place.x + d, nx) for d in range(nx)]
    at_y = [lax.rem(place.y + d, ny) for d in range(ny)]
    low, high = pl.ds(0, HALF), pl.ds(HALF, TILES - HALF)
    core, relays, across, along = {}, {}, {}, []
    for d in order:
        source = parts_ref.at[1 - place.c, :, at_y[d]]
        core[d] = send(source, from_core.at[:, at_y[d]], place.core())
    for d in order:
        core[d].wait()
        sum_core[:, at_y[d]] = parts_ref[place.c, :, at_y[d]] + from_core[:, at_y[d]]
        relays[d] = [
            send(sum_core.at[at_x[2], at_y[d], low], relay_up.at[d], place.along_x(1)),
            send(sum_core.at[at_x[2], at_y[d], high], relay_down.at[d], place.along_x(nx - 1)),
        ]
    for d in order:
        wait_all(relays[d])
        sum_core[at_x[1], at_y[d], low] = sum_core[at_x[1], at_y[d], low] + relay_up[d]
        sum_core[at_x[3], at_y[d], high] = sum_core[at_x[3], at_y[d], high] + relay_down[d]
        across[d] = [
            send(sum_core.at[at_x[1], at_y[d]], from_x.at[0, d], place.along_x(1)),
            send(sum_core.at[at_x[3], at_y[d]], from_x.at[1, d], place.along_x(nx - 1)),
        ]
    for d in order:
        wait_all(across[d])
        sum_x[d] = sum_core[place.x, at_y[d]] + (from_x[0, d] + from_x[1, d])
        if d:
            along.append(send(sum_x.at[d], from_y.at[d - 1], place.along_y(d)))
    wait_all(along)
    sum_y[TILES:nz] = jnp.zeros((nz - TILES, 8, 128), jnp.float32)
    sum_y[0:TILES] = total_of(sum_x[0], from_y, ny - 1)
    copies = [
        send(sum_y.at[lax.rem(place.z + d, nz)], from_z.at[d - 1], place.along_z(d))
        for d in range(1, nz)
    ]
    heads = [
        send(sum_y.at[TILES - 1], head_z.at[d - 1], place.along_z(d)) for d in range(1, nz)
    ]
    wait_all(copies)
    sum_z[...] = total_of(sum_y[place.z], from_z, nz - 1)
    copies = [send(sum_z, got_z.at[d], place.along_z(d)) for d in range(1, nz)]
    chunk_ref[place.z] = sum_z[...]
    wait_all(heads)
    block[...] = total_of(sum_y[TILES - 1], head_z, nz - 1)
    heads = [send(block, block_y.at[d], place.along_y(d)) for d in range(1, ny)]
    block_y[0] = block[...]
    wait_all(heads)
    heads = [send(block_y, block_k.at[d], place.along_k(d)) for d in range(1, 2 * nx)]
    block_k[0] = block_y[...]
    wait_all(copies)
    for d in range(1, nz):
        chunk_ref[lax.rem(place.z - d + nz, nz)] = got_z[d]
    conv = chunk_ref[0:9]
    square[...] = jnp.sum(conv * conv, axis=0)
    squares = [send(square, square_y.at[d - 1], place.along_y(d)) for d in range(1, ny)]
    wait_all(squares)
    part_square[...] = total_of(square[...], square_y, ny - 1)
    squares = [send(part_square, square_k.at[d - 1], place.along_k(d)) for d in range(1, 2 * nx)]
    wait_all(heads)
    spread(place, block_k, gathered_ref)

    def conv_norm():
        wait_all(squares)
        return sum_of(total_of(part_square[...], square_k, 2 * nx - 1))

    return conv_norm


def sum_of(array):
    return jnp.sum(jnp.sum(array, axis=0, keepdims=True), axis=1, keepdims=True)


def dot_highest(left, right):
    return jnp.dot(
        left, right, precision=lax.Precision.HIGHEST, preferred_element_type=jnp.float32
    )


def updates(
    place, samples_all, conv_norm, chunk_ref, gathered_ref, a_factor_ref, g_factor_ref,
    g_inverse_ref, inverse_ref, head_ref, output_ref, precond_ref,
    head_update_ref, conv_update_ref, new_a_ref, new_g_ref,
):
    head_from(place.nx, place.ny, gathered_ref, head_ref, output_ref)
    head_grad = head_ref[...]
    precond = dot_highest(dot_highest(inverse_ref[...], head_grad), g_inverse_ref[...])
    precond_ref[...] = precond
    head_norm = sum_of(precond * head_grad)
    head_scale = -jnp.sqrt(C * NE / 4.0 / head_norm)
    pair = pl.multiple_of(lax.div(place.orb, 2) * 8, 8)
    eight = head_scale * precond_ref[pl.ds(pair, 8), :]
    head_update_ref[...] = jnp.where(place.c == 0, eight, pltpu.roll(eight, 4, 0))[0:4]
    keep = 1.0 - decay_rate
    new_g_ref[...] = decay_rate * g_factor_ref[...] + keep * output_ref[...] / samples_all
    conv_scale = -jnp.sqrt(9 * C * C / 4.0 / conv_norm())
    for half in range(2):
        lanes = slice(128 * half, 128 * half + 128)
        rows = slice(4 * half, 4 * half + 4)
        input_rows = chunk_ref[9][rows]
        new_a_ref[:, lanes] = (
            decay_rate * a_factor_ref[:, lanes] + keep * input_rows / (samples_all * NE)
        )
        inner = conv_scale * chunk_ref[4 * half : 4 * half + 4].reshape(32, 128)
        edge = conv_scale * chunk_ref[8][rows]

        @pl.when(place.c == 0)
        def _(lanes=lanes, inner=inner, edge=edge):
            conv_update_ref[0:32, lanes] = inner
            conv_update_ref[32:36, lanes] = edge

        @pl.when(place.c == 1)
        def _(lanes=lanes, inner=inner, edge=edge):
            conv_update_ref[0:4, lanes] = edge
            conv_update_ref[4:36, lanes] = inner


def step_kernel(
    nx, ny, nz, samples,
    occ_in, energy_in, a_inverse_in, embed_in, conv_w_in, head_w_in,
    a_factor_in, g_factor_in, g_inverse_in,
    head_update_ref, conv_update_ref, new_a_ref, new_g_ref,
    occ_ref, energy_ref, a_inverse_ref, embed_ref, conv_w_ref, head_w_ref,
    a_factor_ref, g_factor_ref, g_inverse_ref,
    rows_own, rows_y, rows_k, energy_own, energy_y, energy_k, energy_z, part_k, part_z,
    embedded_ref, slope_ref, rows_ref, log_ref, cot_ref, pre_ref, rows_t_ref,
    input_ref, output_ref, conv_ref, head_ref, parts_ref, gathered_ref, inverse_ref, precond_ref,
    chunk_ref, *rest,
):
    *buffers, load_sem, send_sem, recv_sem = rest
    place = Place(nx, ny, nz)
    peers = place.signal_peers()
    loads = [
        pltpu.make_async_copy(source, target, load_sem.at[i])
        for i, (source, target) in enumerate(
            [
                (occ_in, occ_ref),
                (energy_in, energy_ref),
                (a_inverse_in, a_inverse_ref),
                (embed_in, embed_ref),
                (conv_w_in, conv_w_ref),
                (head_w_in, head_w_ref),
                (a_factor_in, a_factor_ref),
                (g_factor_in, g_factor_ref),
                (g_inverse_in, g_inverse_ref),
            ]
        )
    ]
    for load in loads:
        load.start()
    send = Sender(send_sem, recv_sem)

    def energy_of(b):
        return jnp.broadcast_to(energy_ref[0:1, b : b + 1], (8, 128))

    def sample(b):
        forward(b, occ_ref, embed_ref, conv_w_ref, head_w_ref,
                embedded_ref, slope_ref, rows_ref, log_ref)

    wait_all(loads[:6])
    energy_own[...] = sum((energy_of(b) for b in range(1, samples)), energy_of(0))
    rows_own[0:4, :] = a_inverse_ref[:, :128]
    rows_own[4:8, :] = a_inverse_ref[:, 128:]
    sample(0)
    place.wait_peers(peers)
    energies = [send(energy_own, energy_y.at[d - 1], place.along_y(d)) for d in range(1, ny)]
    rows = [send(rows_own, rows_y.at[d], place.along_y(d)) for d in range(1, ny)]
    rows_y[0] = rows_own[...]
    sample(1)
    wait_all(energies)
    part_k[...] = total_of(energy_own[...], energy_y, ny - 1)
    energies = [send(part_k, energy_k.at[d - 1], place.along_k(d)) for d in range(1, 2 * nx)]
    wait_all(rows)
    rows = [send(rows_y, rows_k.at[d], place.along_k(d)) for d in range(1, 2 * nx)]
    rows_k[0] = rows_y[...]
    for b in range(2, samples):
        sample(b)
    wait_all(energies)
    part_z[...] = total_of(part_k[...], energy_k, 2 * nx - 1)
    energies = [send(part_z, energy_z.at[d - 1], place.along_z(d)) for d in range(1, nz)]
    for b in range(samples):
        backward(b, occ_ref, head_w_ref, slope_ref, log_ref, cot_ref, pre_ref)
    grams(samples, rows_ref, log_ref, rows_t_ref, input_ref, output_ref)
    wait_all(rows)
    spread(place, rows_k, gathered_ref)
    inverse_from(nx, ny, gathered_ref, inverse_ref)
    wait_all(energies)
    total = total_of(part_z[...], energy_z, nz - 1)[0:1]
    samples_all = samples * 2 * nx * ny * nz
    mean_energy = total / samples_all
    weighted_sums(
        samples,
        lambda b: (energy_of(b)[0:1] - mean_energy) / samples_all,
        embedded_ref, pre_ref, rows_t_ref, cot_ref, conv_ref, head_ref,
    )
    lay_out(nx, ny, conv_ref, input_ref, head_ref, output_ref, parts_ref)
    wait_all(loads[6:])
    conv_norm = exchange(place, send, parts_ref, chunk_ref, gathered_ref, *buffers)
    updates(
        place, samples_all, conv_norm, chunk_ref, gathered_ref, a_factor_ref, g_factor_ref, g_inverse_ref,
        inverse_ref, head_ref, output_ref, precond_ref,
        head_update_ref, conv_update_ref, new_a_ref, new_g_ref,
    )


def per_device(
    nx,
    ny,
    nz,
    occupations,
    local_energy,
    embed_weight,
    conv_weight,
    head_weight,
    a_factor,
    g_factor,
    a_inverse,
    g_inverse,
):
    samples = occupations.shape[0]
    sites = L * L
    orb = 2 * nx * ny
    copies = 2 * (ny - 1) + 2 * (2 * nx - 1) + nz - 1
    copies += 5 * ny + 3 * (ny - 1) + 3 * (nz - 1) + 2 * (2 * nx - 1)

    inputs = (
        occupations,
        local_energy.reshape(1, samples),
        a_inverse,
        embed_weight,
        conv_weight,
        head_weight,
        a_factor,
        g_factor,
        g_inverse,
    )

    def buffer(*shape, dtype=jnp.float32):
        return pltpu.VMEM(shape, dtype)

    def tiles(*lead):
        return pltpu.VMEM(lead + (8, 128), jnp.float32)

    return pl.pallas_call(
        functools.partial(step_kernel, nx, ny, nz, samples),
        name="natural_step",
        out_shape=(
            jax.ShapeDtypeStruct((C // orb, NE), jnp.float32),
            jax.ShapeDtypeStruct((9 * C // orb, C), jnp.float32),
            jax.ShapeDtypeStruct((C // orb, C), jnp.float32),
            jax.ShapeDtypeStruct((NE, NE), jnp.float32),
        ),
        in_specs=[pl.BlockSpec(memory_space=pl.ANY)] * 9,
        out_specs=[pl.BlockSpec(memory_space=pltpu.VMEM)] * 4,
        scratch_shapes=[pltpu.VMEM(a.shape, a.dtype) for a in inputs]
        + [
            tiles(),
            tiles(ny),
            tiles(2 * nx, ny),
            tiles(),
            tiles(ny - 1),
            tiles(2 * nx - 1),
            tiles(nz - 1),
            tiles(),
            tiles(),
            buffer(samples, sites, C, dtype=jnp.bfloat16),
            buffer(samples, sites, C),
            buffer(samples, NE, C, dtype=jnp.bfloat16),
            buffer(samples, NE, NE),
            buffer(samples, NE, NE, dtype=jnp.bfloat16),
            buffer(samples, sites, C, dtype=jnp.bfloat16),
            buffer(C, samples * NE, dtype=jnp.bfloat16),
            buffer(C, C),
            buffer(NE, NE),
            buffer(9 * C, C),
            buffer(C, NE),
            tiles(2, nx, ny, TILES),
            tiles(2 * nx, ny),
            buffer(C, C),
            buffer(C, NE),
            tiles(nz),
            tiles(nx, ny, TILES),
            tiles(nx, ny, TILES),
            tiles(ny, HALF),
            tiles(ny, TILES - HALF),
            tiles(2, ny, TILES),
            tiles(ny, TILES),
            tiles(ny - 1, TILES),
            tiles(nz),
            tiles(nz - 1),
            tiles(),
            tiles(nz),
            tiles(nz - 1),
            tiles(),
            tiles(ny),
            tiles(2 * nx, ny),
            tiles(),
            tiles(ny - 1),
            tiles(),
            tiles(2 * nx - 1),
            pltpu.SemaphoreType.DMA((len(inputs),)),
            pltpu.SemaphoreType.DMA((copies,)),
            pltpu.SemaphoreType.DMA((copies,)),
        ],
        compiler_params=pltpu.CompilerParams(collective_id=0, has_side_effects=True),
    )(*inputs)


def solution(mesh):
    nz, orb = mesh.shape["walker"], mesh.shape["orb"]
    in_specs = (
        P(("walker", "orb"), None),
        P(("walker", "orb")),
        P(),
        P(),
        P(),
        P("orb", None),
        P(),
        P("orb", None),
        P(),
    )
    out_specs = (P("orb", None), P("orb", None), P("orb", None), P())
    return jax.shard_map(
        functools.partial(per_device, X_CHIPS, orb // (2 * X_CHIPS), nz),
        mesh=mesh,
        in_specs=in_specs,
        out_specs=out_specs,
        check_vma=False,
    )
```

```python
import functools
import math

import jax
import jax.numpy as jnp
from jax import lax
from jax.experimental import pallas as pl
from jax.experimental.pallas import tpu as pltpu
from jax.sharding import PartitionSpec as P

L = 16
C = 256
NS_STEPS = 3
NE = 128
X_CHIPS = 4
TILES = 11
HALF = 6

decay_rate = 0.8
MESH = pl.DeviceIdType.MESH


class Place:
    def __init__(self, nx, ny, nz):
        self.nx, self.ny, self.nz = nx, ny, nz
        self.z = lax.axis_index("walker")
        self.orb = lax.axis_index("orb")
        self.c = lax.rem(self.orb, 2)
        self.y = lax.rem(lax.div(self.orb, 2), ny)
        self.x = lax.div(self.orb, 2 * ny)
        self.k = self.x * 2 + self.c

    def at(self, x, y, c):
        return (self.z, (x * self.ny + y) * 2 + c)

    def core(self):
        return self.at(self.x, self.y, 1 - self.c)

    def along_x(self, d):
        return self.at(lax.rem(self.x + d, self.nx), self.y, self.c)

    def along_y(self, d):
        return self.at(self.x, lax.rem(self.y + d, self.ny), self.c)

    def along_k(self, d):
        k = lax.rem(self.k + d, 2 * self.nx)
        return self.at(lax.div(k, 2), self.y, lax.rem(k, 2))

    def along_z(self, d):
        return (lax.rem(self.z + d, self.nz), self.orb)

    def signal_peers(self):
        barrier = pltpu.get_barrier_semaphore()
        peers = [self.along_y(d) for d in range(1, self.ny)]
        peers += [self.along_k(d) for d in range(1, 2 * self.nx)]
        peers += [self.along_z(d) for d in range(1, self.nz)]
        for peer in peers:
            pl.semaphore_signal(barrier, inc=1, device_id=peer, device_id_type=MESH)
        return len(peers)

    def wait_peers(self, count):
        pl.semaphore_wait(pltpu.get_barrier_semaphore(), count)


class Sender:
    def __init__(self, send_sem, recv_sem):
        self.send_sem, self.recv_sem, self.used = send_sem, recv_sem, 0

    def __call__(self, source, target, device):
        copy = pltpu.make_async_remote_copy(
            src_ref=source,
            dst_ref=target,
            send_sem=self.send_sem.at[self.used],
            recv_sem=self.recv_sem.at[self.used],
            device_id=device,
            device_id_type=MESH,
        )
        copy.start()
        self.used += 1
        return copy


def wait_all(copies):
    for copy in copies:
        copy.wait()


def total_of(first, ref, count):
    total = first
    for i in range(count):
        total = total + ref[i]
    return total


def spread(place, slots_ref, out_ref):
    for i in range(2 * place.nx):
        k = lax.rem(place.k - i + 2 * place.nx, 2 * place.nx)
        for j in range(place.ny):
            y = lax.rem(place.y - j + place.ny, place.ny)
            out_ref[k, y] = slots_ref[i, j]


def site_shift_y(field, b):
    if b == 0:
        return field
    y = lax.broadcasted_iota(jnp.int32, field.shape, 0) & (L - 1)
    sites = field.shape[0]
    if b == 1:
        edge, inside = pltpu.roll(field, L - 1, 0), pltpu.roll(field, sites - 1, 0)
        return jnp.where(y == L - 1, edge, inside)
    edge, inside = pltpu.roll(field, sites - L + 1, 0), pltpu.roll(field, 1, 0)
    return jnp.where(y == 0, edge, inside)


def site_shift_x(field, a):
    if a == 0:
        return field
    cut = L if a == 1 else field.shape[0] - L
    return jnp.concatenate([field[cut:], field[:cut]], axis=0)


def site_patches(field, sign):
    by_y = {b: site_shift_y(field, sign * b).astype(jnp.bfloat16) for b in (-1, 0, 1)}
    return jnp.concatenate(
        [site_shift_x(by_y[b], sign * a) for a in (-1, 0, 1) for b in (-1, 0, 1)], axis=1
    )


def multiply(left, right):
    return jnp.dot(
        left.astype(jnp.bfloat16), right.astype(jnp.bfloat16), preferred_element_type=jnp.float32
    )


def electrons_by_site(occ_ref, b):
    sites = lax.broadcasted_iota(jnp.int32, (L * L, NE), 0)
    return (sites == occ_ref[b : b + 1, :]).astype(jnp.float32)


def forward(b, occ_ref, embed_ref, conv_w_ref, head_w_ref,
            embedded_ref, slope_ref, rows_ref, log_ref):
    by_site = electrons_by_site(occ_ref, b)
    electron = lax.broadcasted_iota(jnp.int32, (NE, 128), 0)
    lane = lax.broadcasted_iota(jnp.int32, (NE, 128), 1)
    down = (electron >= NE // 2).astype(jnp.int32)
    spin = ((lane & 1) == down).astype(jnp.float32)
    counts = multiply(by_site, spin)
    tap_of_lane = lax.broadcasted_iota(jnp.int32, counts.shape, 1) >> 1
    near = jnp.zeros_like(counts)
    for j in (-1, 0, 1):
        at_y = site_shift_y(counts, j)
        for i in (-1, 0, 1):
            tap = (i + 1) * 3 + j + 1
            near = jnp.where(tap_of_lane == tap, site_shift_x(at_y, i), near)
    embedded = jnp.tanh(multiply(near[:, : embed_ref.shape[0]], embed_ref[...])).astype(jnp.bfloat16)
    embedded_ref[b] = embedded
    wide = embedded.astype(jnp.float32)
    squash = jnp.tanh(multiply(site_patches(wide, 1), conv_w_ref[...]))
    slope_ref[b] = 1.0 - squash * squash
    hidden = (wide + squash).astype(jnp.bfloat16)
    rows = multiply(by_site.T, hidden).astype(jnp.bfloat16)
    rows_ref[b] = rows
    orbital_tanh = jnp.tanh(multiply(rows, head_w_ref[...]))
    shift = (0.35 / math.sqrt(NE)) * orbital_tanh
    row = lax.broadcasted_iota(jnp.int32, (NE, NE), 0)
    column = lax.broadcasted_iota(jnp.int32, (NE, NE), 1)
    identity = (row == column).astype(jnp.float32)
    second = multiply(shift, shift)
    inverse_est = identity - shift + second - multiply(shift, second)
    inverse_est = inverse_est + multiply(inverse_est, multiply(second, second))
    log_ref[b] = (1.0 - orbital_tanh * orbital_tanh) * inverse_est.T


def backward(b, occ_ref, head_w_ref, slope_ref, log_ref, cot_ref, pre_ref):
    cotangent = ((0.35 / math.sqrt(NE)) * log_ref[b]).astype(jnp.bfloat16)
    cot_ref[b] = cotangent
    row_grads = lax.dot_general(
        cotangent, head_w_ref[...], (((1,), (1,)), ((), ())), preferred_element_type=jnp.float32
    ).astype(jnp.bfloat16)
    hidden_grad = multiply(electrons_by_site(occ_ref, b), row_grads)
    pre_ref[b] = (hidden_grad * slope_ref[b]).astype(jnp.bfloat16)


def grams(samples, rows_ref, log_ref, rows_t_ref, input_ref, output_ref):
    rows = rows_ref[...].reshape(samples * NE, C)
    rows_t = rows.astype(jnp.float32).T.astype(jnp.bfloat16)
    rows_t_ref[...] = rows_t
    input_ref[...] = multiply(rows_t, rows)
    logs = log_ref[...].reshape(samples * NE, NE)
    output_ref[...] = jnp.dot(
        logs.T, logs, precision=lax.Precision.HIGHEST, preferred_element_type=jnp.float32
    )


def weighted_sums(samples, weight_of, embedded_ref, pre_ref, rows_t_ref, cot_ref, conv_ref, head_ref):
    for b in range(samples):
        weight = weight_of(b)
        wide = jnp.concatenate([weight, weight], axis=1)
        embedded_t = embedded_ref[b].astype(jnp.float32).T
        terms = multiply(embedded_t, site_patches(pre_ref[b].astype(jnp.float32), -1))
        head = weight * multiply(rows_t_ref[:, b * NE : (b + 1) * NE], cot_ref[b])
        head_ref[...] = head if b == 0 else head_ref[...] + head
        for tap in range(9):
            rows = slice(tap * C, (tap + 1) * C)
            term = wide * terms[:, rows]
            conv_ref[rows, :] = term if b == 0 else conv_ref[rows, :] + term


def lay_out(nx, ny, conv_ref, input_ref, head_ref, output_ref, parts_ref, ready):
    row = lax.broadcasted_iota(jnp.int32, (8, 128), 0)

    def halves(first, second, c):
        if c == 0:
            return jnp.where(row < 4, first, pltpu.roll(second, 4, 0))
        return jnp.where(row < 4, pltpu.roll(first, 4, 0), second)

    for y, x in [(y, x) for y in range(ny) for x in range(nx)]:
        pair = x * ny + y
        for c in range(2):
            top = 72 * pair + 40 * c
            for half in range(2):
                lanes = slice(128 * half, 128 * half + 128)
                for i in range(4):
                    tile = conv_ref[top + 8 * i : top + 8 * i + 8, lanes]
                    parts_ref[c, x, y, 4 * half + i] = tile
            middle = slice(72 * pair + 32, 72 * pair + 40)
            parts_ref[c, x, y, 8] = halves(conv_ref[middle, :128], conv_ref[middle, 128:], c)
            eight = slice(8 * pair, 8 * pair + 8)
            parts_ref[c, x, y, 9] = halves(input_ref[eight, :128], input_ref[eight, 128:], c)
            place = 4 * (pair % 2) + 2 * c
            output = output_ref[8 * (pair // 2) : 8 * (pair // 2) + 8, :]
            output = pltpu.roll(output, (4 - place) % 8, 0) if place != 4 else output
            head = head_ref[eight, :] if c == 0 else pltpu.roll(head_ref[eight, :], 4, 0)
            parts_ref[c, x, y, 10] = jnp.where(row < 4, head, output)
        if x == nx - 1:
            ready(y)


def row_index():
    return lax.broadcasted_iota(jnp.int32, (8, 128), 0)


def inverse_from(nx, ny, gathered_ref, inverse_ref):
    row = row_index()
    for pair in range(nx * ny):
        x, y = pair // ny, pair % ny
        first, second = gathered_ref[2 * x, y], gathered_ref[2 * x + 1, y]
        eight = slice(8 * pair, 8 * pair + 8)
        inverse_ref[eight, :128] = jnp.where(row < 4, first, pltpu.roll(second, 4, 0))
        inverse_ref[eight, 128:] = jnp.where(row < 4, pltpu.roll(first, 4, 0), second)


def head_from(nx, ny, gathered_ref, head_ref, output_ref):
    row = row_index()
    for pair in range(0, nx * ny, 2):
        tiles = []
        for p in (pair, pair + 1):
            x, y = p // ny, p % ny
            first, second = gathered_ref[2 * x, y], gathered_ref[2 * x + 1, y]
            head_ref[8 * p : 8 * p + 8, :] = jnp.where(row < 4, first, pltpu.roll(second, 4, 0))
            tiles += [first, second]
        upper = jnp.where(row < 2, pltpu.roll(tiles[0], 4, 0), pltpu.roll(tiles[1], 6, 0))
        lower = jnp.where(row < 6, tiles[2], pltpu.roll(tiles[3], 2, 0))
        output_ref[4 * pair : 4 * pair + 8, :] = jnp.where(row < 4, upper, lower)


def exchange(
    place, send, core, parts_ref, chunk_ref, gathered_ref,
    from_core, sum_core, relay_up, relay_down, from_x, sum_x, from_y, sum_y, from_z, sum_z, got_z,
    head_z, block, block_y, block_k, square, square_y, part_square, square_k,
):
    nx, ny, nz = place.nx, place.ny, place.nz
    order = sorted(range(1, ny), key=lambda d: -min(d, ny - d)) + [0]
    at_x = [lax.rem(place.x + d, nx) for d in range(nx)]
    at_y = [lax.rem(place.y + d, ny) for d in range(ny)]
    low, high = pl.ds(0, HALF), pl.ds(HALF, TILES - HALF)
    relays, across, along = {}, {}, []
    wait_all(core)
    for d in order:
        sum_core[:, at_y[d]] = parts_ref[place.c, :, at_y[d]] + from_core[:, at_y[d]]
        relays[d] = [
            send(sum_core.at[at_x[2], at_y[d], low], relay_up.at[d], place.along_x(1)),
            send(sum_core.at[at_x[2], at_y[d], high], relay_down.at[d], place.along_x(nx - 1)),
        ]
    for d in order:
        wait_all(relays[d])
        sum_core[at_x[1], at_y[d], low] = sum_core[at_x[1], at_y[d], low] + relay_up[d]
        sum_core[at_x[3], at_y[d], high] = sum_core[at_x[3], at_y[d], high] + relay_down[d]
        across[d] = [
            send(sum_core.at[at_x[1], at_y[d]], from_x.at[0, d], place.along_x(1)),
            send(sum_core.at[at_x[3], at_y[d]], from_x.at[1, d], place.along_x(nx - 1)),
        ]
    for d in order:
        wait_all(across[d])
        sum_x[d] = sum_core[place.x, at_y[d]] + (from_x[0, d] + from_x[1, d])
        if d:
            along.append(send(sum_x.at[d], from_y.at[d - 1], place.along_y(d)))
    wait_all(along)
    sum_y[TILES:nz] = jnp.zeros((nz - TILES, 8, 128), jnp.float32)
    sum_y[0:TILES] = total_of(sum_x[0], from_y, ny - 1)
    copies = [
        send(sum_y.at[lax.rem(place.z + d, nz)], from_z.at[d - 1], place.along_z(d))
        for d in range(1, nz)
    ]
    heads = [
        send(sum_y.at[TILES - 1], head_z.at[d - 1], place.along_z(d)) for d in range(1, nz)
    ]
    wait_all(copies)
    sum_z[...] = total_of(sum_y[place.z], from_z, nz - 1)
    copies = [send(sum_z, got_z.at[d], place.along_z(d)) for d in range(1, nz)]
    chunk_ref[place.z] = sum_z[...]
    wait_all(heads)
    block[...] = total_of(sum_y[TILES - 1], head_z, nz - 1)
    heads = [send(block, block_y.at[d], place.along_y(d)) for d in range(1, ny)]
    block_y[0] = block[...]
    wait_all(heads)
    heads = [send(block_y, block_k.at[d], place.along_k(d)) for d in range(1, 2 * nx)]
    block_k[0] = block_y[...]
    wait_all(copies)
    for d in range(1, nz):
        chunk_ref[lax.rem(place.z - d + nz, nz)] = got_z[d]
    conv = chunk_ref[0:9]
    square[...] = jnp.sum(conv * conv, axis=0)
    squares = [send(square, square_y.at[d - 1], place.along_y(d)) for d in range(1, ny)]
    wait_all(squares)
    part_square[...] = total_of(square[...], square_y, ny - 1)
    squares = [send(part_square, square_k.at[d - 1], place.along_k(d)) for d in range(1, 2 * nx)]
    wait_all(heads)
    spread(place, block_k, gathered_ref)

    def conv_norm():
        wait_all(squares)
        return sum_of(total_of(part_square[...], square_k, 2 * nx - 1))

    return conv_norm


def sum_of(array):
    return jnp.sum(jnp.sum(array, axis=0, keepdims=True), axis=1, keepdims=True)


def dot_highest(left, right):
    return jnp.dot(
        left, right, precision=lax.Precision.HIGHEST, preferred_element_type=jnp.float32
    )


def updates(
    place, samples_all, conv_norm, chunk_ref, gathered_ref, a_factor_ref, g_factor_ref,
    g_inverse_ref, inverse_ref, head_ref, output_ref, precond_ref,
    head_update_ref, conv_update_ref, new_a_ref, new_g_ref,
):
    head_from(place.nx, place.ny, gathered_ref, head_ref, output_ref)
    head_grad = head_ref[...]
    precond = dot_highest(dot_highest(inverse_ref[...], head_grad), g_inverse_ref[...])
    precond_ref[...] = precond
    head_norm = sum_of(precond * head_grad)
    head_scale = -jnp.sqrt(C * NE / 4.0 / head_norm)
    pair = pl.multiple_of(lax.div(place.orb, 2) * 8, 8)
    eight = head_scale * precond_ref[pl.ds(pair, 8), :]
    head_update_ref[...] = jnp.where(place.c == 0, eight, pltpu.roll(eight, 4, 0))[0:4]
    keep = 1.0 - decay_rate
    new_g_ref[...] = decay_rate * g_factor_ref[...] + keep * output_ref[...] / samples_all
    conv_scale = -jnp.sqrt(9 * C * C / 4.0 / conv_norm())
    for half in range(2):
        lanes = slice(128 * half, 128 * half + 128)
        rows = slice(4 * half, 4 * half + 4)
        input_rows = chunk_ref[9][rows]
        new_a_ref[:, lanes] = (
            decay_rate * a_factor_ref[:, lanes] + keep * input_rows / (samples_all * NE)
        )
        inner = conv_scale * chunk_ref[4 * half : 4 * half + 4].reshape(32, 128)
        edge = conv_scale * chunk_ref[8][rows]

        @pl.when(place.c == 0)
        def _(lanes=lanes, inner=inner, edge=edge):
            conv_update_ref[0:32, lanes] = inner
            conv_update_ref[32:36, lanes] = edge

        @pl.when(place.c == 1)
        def _(lanes=lanes, inner=inner, edge=edge):
            conv_update_ref[0:4, lanes] = edge
            conv_update_ref[4:36, lanes] = inner


def step_kernel(
    nx, ny, nz, samples,
    occ_in, energy_in, a_inverse_in, embed_in, conv_w_in, head_w_in,
    a_factor_in, g_factor_in, g_inverse_in,
    head_update_ref, conv_update_ref, new_a_ref, new_g_ref,
    occ_ref, energy_ref, a_inverse_ref, embed_ref, conv_w_ref, head_w_ref,
    a_factor_ref, g_factor_ref, g_inverse_ref,
    rows_own, rows_y, rows_k, energy_own, energy_y, energy_k, energy_z, part_k, part_z,
    embedded_ref, slope_ref, rows_ref, log_ref, cot_ref, pre_ref, rows_t_ref,
    input_ref, output_ref, conv_ref, head_ref, parts_ref, gathered_ref, inverse_ref, precond_ref,
    chunk_ref, *rest,
):
    *buffers, load_sem, send_sem, recv_sem = rest
    place = Place(nx, ny, nz)
    peers = place.signal_peers()
    loads = [
        pltpu.make_async_copy(source, target, load_sem.at[i])
        for i, (source, target) in enumerate(
            [
                (occ_in, occ_ref),
                (energy_in, energy_ref),
                (a_inverse_in, a_inverse_ref),
                (embed_in, embed_ref),
                (conv_w_in, conv_w_ref),
                (head_w_in, head_w_ref),
                (a_factor_in, a_factor_ref),
                (g_factor_in, g_factor_ref),
                (g_inverse_in, g_inverse_ref),
            ]
        )
    ]
    for load in loads:
        load.start()
    send = Sender(send_sem, recv_sem)

    def energy_of(b):
        return jnp.broadcast_to(energy_ref[0:1, b : b + 1], (8, 128))

    def sample(b):
        forward(b, occ_ref, embed_ref, conv_w_ref, head_w_ref,
                embedded_ref, slope_ref, rows_ref, log_ref)

    wait_all(loads[:6])
    energy_own[...] = sum((energy_of(b) for b in range(1, samples)), energy_of(0))
    rows_own[0:4, :] = a_inverse_ref[:, :128]
    rows_own[4:8, :] = a_inverse_ref[:, 128:]
    sample(0)
    place.wait_peers(peers)
    energies = [send(energy_own, energy_y.at[d - 1], place.along_y(d)) for d in range(1, ny)]
    rows = [send(rows_own, rows_y.at[d], place.along_y(d)) for d in range(1, ny)]
    rows_y[0] = rows_own[...]
    sample(1)
    wait_all(energies)
    part_k[...] = total_of(energy_own[...], energy_y, ny - 1)
    energies = [send(part_k, energy_k.at[d - 1], place.along_k(d)) for d in range(1, 2 * nx)]
    wait_all(rows)
    rows = [send(rows_y, rows_k.at[d], place.along_k(d)) for d in range(1, 2 * nx)]
    rows_k[0] = rows_y[...]
    for b in range(2, samples):
        sample(b)
    wait_all(energies)
    part_z[...] = total_of(part_k[...], energy_k, 2 * nx - 1)
    energies = [send(part_z, energy_z.at[d - 1], place.along_z(d)) for d in range(1, nz)]
    for b in range(samples):
        backward(b, occ_ref, head_w_ref, slope_ref, log_ref, cot_ref, pre_ref)
    grams(samples, rows_ref, log_ref, rows_t_ref, input_ref, output_ref)
    wait_all(rows)
    spread(place, rows_k, gathered_ref)
    inverse_from(nx, ny, gathered_ref, inverse_ref)
    wait_all(energies)
    total = total_of(part_z[...], energy_z, nz - 1)[0:1]
    samples_all = samples * 2 * nx * ny * nz
    mean_energy = total / samples_all
    weighted_sums(
        samples,
        lambda b: (energy_of(b)[0:1] - mean_energy) / samples_all,
        embedded_ref, pre_ref, rows_t_ref, cot_ref, conv_ref, head_ref,
    )
    core = []

    def send_core(y):
        source, target = parts_ref.at[1 - place.c, :, y], buffers[0].at[:, y]
        core.append(send(source, target, place.core()))

    lay_out(nx, ny, conv_ref, input_ref, head_ref, output_ref, parts_ref, send_core)
    wait_all(loads[6:])
    conv_norm = exchange(place, send, core, parts_ref, chunk_ref, gathered_ref, *buffers)
    updates(
        place, samples_all, conv_norm, chunk_ref, gathered_ref, a_factor_ref, g_factor_ref, g_inverse_ref,
        inverse_ref, head_ref, output_ref, precond_ref,
        head_update_ref, conv_update_ref, new_a_ref, new_g_ref,
    )


def per_device(
    nx,
    ny,
    nz,
    occupations,
    local_energy,
    embed_weight,
    conv_weight,
    head_weight,
    a_factor,
    g_factor,
    a_inverse,
    g_inverse,
):
    samples = occupations.shape[0]
    sites = L * L
    orb = 2 * nx * ny
    copies = 2 * (ny - 1) + 2 * (2 * nx - 1) + nz - 1
    copies += 5 * ny + 3 * (ny - 1) + 3 * (nz - 1) + 2 * (2 * nx - 1)

    inputs = (
        occupations,
        local_energy.reshape(1, samples),
        a_inverse,
        embed_weight,
        conv_weight,
        head_weight,
        a_factor,
        g_factor,
        g_inverse,
    )

    def buffer(*shape, dtype=jnp.float32):
        return pltpu.VMEM(shape, dtype)

    def tiles(*lead):
        return pltpu.VMEM(lead + (8, 128), jnp.float32)

    return pl.pallas_call(
        functools.partial(step_kernel, nx, ny, nz, samples),
        name="natural_step",
        out_shape=(
            jax.ShapeDtypeStruct((C // orb, NE), jnp.float32),
            jax.ShapeDtypeStruct((9 * C // orb, C), jnp.float32),
            jax.ShapeDtypeStruct((C // orb, C), jnp.float32),
            jax.ShapeDtypeStruct((NE, NE), jnp.float32),
        ),
        in_specs=[pl.BlockSpec(memory_space=pl.ANY)] * 9,
        out_specs=[pl.BlockSpec(memory_space=pltpu.VMEM)] * 4,
        scratch_shapes=[pltpu.VMEM(a.shape, a.dtype) for a in inputs]
        + [
            tiles(),
            tiles(ny),
            tiles(2 * nx, ny),
            tiles(),
            tiles(ny - 1),
            tiles(2 * nx - 1),
            tiles(nz - 1),
            tiles(),
            tiles(),
            buffer(samples, sites, C, dtype=jnp.bfloat16),
            buffer(samples, sites, C),
            buffer(samples, NE, C, dtype=jnp.bfloat16),
            buffer(samples, NE, NE),
            buffer(samples, NE, NE, dtype=jnp.bfloat16),
            buffer(samples, sites, C, dtype=jnp.bfloat16),
            buffer(C, samples * NE, dtype=jnp.bfloat16),
            buffer(C, C),
            buffer(NE, NE),
            buffer(9 * C, C),
            buffer(C, NE),
            tiles(2, nx, ny, TILES),
            tiles(2 * nx, ny),
            buffer(C, C),
            buffer(C, NE),
            tiles(nz),
            tiles(nx, ny, TILES),
            tiles(nx, ny, TILES),
            tiles(ny, HALF),
            tiles(ny, TILES - HALF),
            tiles(2, ny, TILES),
            tiles(ny, TILES),
            tiles(ny - 1, TILES),
            tiles(nz),
            tiles(nz - 1),
            tiles(),
            tiles(nz),
            tiles(nz - 1),
            tiles(),
            tiles(ny),
            tiles(2 * nx, ny),
            tiles(),
            tiles(ny - 1),
            tiles(),
            tiles(2 * nx - 1),
            pltpu.SemaphoreType.DMA((len(inputs),)),
            pltpu.SemaphoreType.DMA((copies,)),
            pltpu.SemaphoreType.DMA((copies,)),
        ],
        compiler_params=pltpu.CompilerParams(collective_id=0, has_side_effects=True),
    )(*inputs)


def solution(mesh):
    nz, orb = mesh.shape["walker"], mesh.shape["orb"]
    in_specs = (
        P(("walker", "orb"), None),
        P(("walker", "orb")),
        P(),
        P(),
        P(),
        P("orb", None),
        P(),
        P("orb", None),
        P(),
    )
    out_specs = (P("orb", None), P("orb", None), P("orb", None), P())
    return jax.shard_map(
        functools.partial(per_device, X_CHIPS, orb // (2 * X_CHIPS), nz),
        mesh=mesh,
        in_specs=in_specs,
        out_specs=out_specs,
        check_vma=False,
    )
```
